128 devices in a mesh: seq: 4 (over z), tp: 32 (over y, x, core).
Axes of the slice: x: 4, y: 4, z: 4, core: 2. Of those that a mesh axis runs over, the one named last changes fastest.
Arguments:
- residual: bfloat16 [8192, 2048], P('seq', 'tp'), may hold values from -6 to 6
- attn_gain: bfloat16 [2048], replicated, may hold values from 0.25 to 1.75
- attn_in: bfloat16 [3, 2048, 2048], P(None, None, 'tp')
- attn_out: bfloat16 [2048, 2048], P('tp'), may hold values from -0.125 to 0.125
- ffn_gain: bfloat16 [2048], replicated, may hold values from 0.25 to 1.75
- ffn_in: bfloat16 [2, 2048, 20480], P(None, None, 'tp'), may hold values from -0.125 to 0.125
- ffn_out: bfloat16 [20480, 2048], P('tp'), may hold values from -0.0390625 to 0.0390625
- route_rows: int32 [4, 224], P('seq'), may hold values from 0 to 2047, as said below
- route_counts: int32 [4], replicated, may hold values from 1 to 224, 512 in all
Outputs:
- layer_out: bfloat16 [8192, 2048], P('seq', 'tp')
The draws below stay inside these ranges and needn't reach their ends.
Inputs may be any that keep to these rules, and one draw needn't show every extreme that they name: `route_rows`: in each row s the 224 entries are distinct positions of that shard; only the first route_counts[s] entries are used; each row holds 0 and 2047. `route_counts`: the counts sum to 512 and the largest is exactly 224.
All inputs are finite; a program needn't handle non-finite values.
Results may differ from the reference program's by a relative error of at most 0.014.
Values may be sent and summed in bfloat16 or wider, within the bound.
A program may use at most 64 MiB of HBM per device.

```python
import math
import jax
import jax.numpy as jnp
import numpy as np
from jax import lax

D = 2048
HEADS = 32
HD = 64
FF = 20480
TOK_SEQ = 2048
RADIUS = 127
TOKENS = 8192
ROUTED = 512
CAP = 224
N_SEQ = 4
N_TP = 32


def draw_attn_in(key, part):
    key_list = jax.random.split(jax.random.fold_in(key, 11), 1)
    base_draw = jax.random.normal(key_list[0], (3, D, D), jnp.float32) / D ** 0.5
    return base_draw.astype(jnp.bfloat16)


def draw_route_rows(key, part):

    def one_shard(shard_key):
        first_key, second_key = jax.random.split(shard_key)
        middle = jax.random.permutation(first_key, TOK_SEQ - 2)[:CAP - 2].astype(jnp.int32) + 1
        picked = jnp.concatenate([jnp.array([0, TOK_SEQ - 1], jnp.int32), middle])
        return jax.random.permutation(second_key, picked)
    return jax.vmap(one_shard)(jax.random.split(jax.random.fold_in(key, 23), N_SEQ))


def shard_levels(stream_key, shape, cuts, least, top_value):
    gain, own = 1.0, jax.random.fold_in(stream_key, 6)
    for dim, blocks in cuts:
        draws = jnp.exp(jax.random.uniform(jax.random.fold_in(own, dim), (blocks,), jnp.float32, least / len(cuts), top_value / len(cuts)))
        gain = gain * jnp.repeat(draws, shape[dim] // blocks).reshape([-1 if axis == dim else 1 for axis in range(len(shape))])
    return gain


def split_up(count, total, bound, lean):
    loads = [(1 << 20) // math.isqrt(rank ** lean) + 1 for rank in range(2, count + 1)]
    rest, given = total - bound - (count - 1), [1] * (count - 1)
    while rest > 0:
        free = [i for i in range(count - 1) if given[i] < bound]
        whole, left = sum([loads[i] for i in free]), rest
        for i in free:
            more = min(bound - given[i], max(1, left * loads[i] // whole), rest)
            given[i] = given[i] + more
            rest = rest - more
    return np.array([bound] + given)


def ragged_sizes(own_key, amount, total, limit, skew):
    if amount == 2:
        one = jax.random.randint(own_key, (), max(1, total - limit), min(limit, total - 1) + 1)
        return jnp.stack([one, total - one])
    tallies = jnp.asarray(split_up(amount, total, limit, skew), jnp.int32)
    pairs = (amount - 1) // 2
    source_of, sink = tallies[1:1 + 2 * pairs:2], tallies[2:2 + 2 * pairs:2]
    margin = jnp.minimum(source_of - 1, limit - sink)
    shifted = jax.random.randint(jax.random.fold_in(own_key, 1), (pairs,), 0, 1 << 20) % (margin + 1)
    tallies = tallies.at[1:1 + 2 * pairs:2].set(source_of - shifted).at[2:2 + 2 * pairs:2].set(sink + shifted)
    return tallies[jax.random.permutation(jax.random.fold_in(own_key, 2), amount)]


def centred(stream_key, shape, spread, reach, shards=(), held_as=jnp.bfloat16):
    drawn = jax.random.normal(stream_key, shape, jnp.float32) * spread
    if len(shards) > 0:
        drawn = shard_levels(stream_key, shape, shards, -0.22, 0.18) * drawn
    return jnp.clip(drawn, min=-reach, max=reach).astype(held_as)


def setup_inputs(seed: int = 0) -> dict:
    seeds = jax.random.split(jax.random.key(seed), 10)
    residual = centred(seeds[0], (TOKENS, D), 1.0, 6.0, ((0, 4), (1, 32)))
    attn_gain = jnp.clip(1.0 + 0.15 * jax.random.normal(seeds[1], (D,), jnp.float32), 0.25, 1.75).astype(jnp.bfloat16)
    attn_in = draw_attn_in(jax.random.fold_in(seeds[9], 71), 0)
    attn_out = centred(seeds[3], (D, D), D ** -0.5, 0.125, ((0, 32),))
    ffn_gain = jnp.clip(1.0 + 0.15 * jax.random.normal(seeds[4], (D,), jnp.float32), 0.25, 1.75).astype(jnp.bfloat16)
    ffn_in = centred(seeds[5], (2, D, FF), D ** -0.5, 0.125, ((2, 32),))
    ffn_out = centred(seeds[6], (FF, D), FF ** -0.5, 0.0390625, ((0, 32),))
    route_rows = draw_route_rows(jax.random.fold_in(seeds[9], 71), 0)
    route_counts = ragged_sizes(seeds[8], N_SEQ, ROUTED, CAP, 2).astype(jnp.int32)
    return {"residual": residual, "attn_gain": attn_gain, "attn_in": attn_in, "attn_out": attn_out, "ffn_gain": ffn_gain, "ffn_in": ffn_in, "ffn_out": ffn_out, "route_rows": route_rows, "route_counts": route_counts}


epsilon = 1e-06

def rms_norm(values, gain_row):
    wide = values.astype(jnp.float32)
    mean_square = lax.optimization_barrier(jnp.mean(wide * wide, axis=-1, keepdims=True))
    return (wide * lax.rsqrt(mean_square + epsilon) * gain_row.astype(jnp.float32)).astype(jnp.bfloat16)

def reference(residual, attn_gain, attn_in, attn_out, ffn_gain, ffn_in, ffn_out, route_rows, route_counts):
    length = TOKENS
    block = min(512, TOK_SEQ)
    span = block + 2 * RADIUS
    normed = rms_norm(residual, attn_gain)
    query_rows = jnp.dot(normed, attn_in[0], preferred_element_type=jnp.float32).astype(jnp.bfloat16).reshape(length, HEADS, HD)
    key_rows = jnp.dot(normed, attn_in[1], preferred_element_type=jnp.float32).astype(jnp.bfloat16).reshape(length, HEADS, HD)
    value_rows = jnp.dot(normed, attn_in[2], preferred_element_type=jnp.float32).astype(jnp.bfloat16).reshape(length, HEADS, HD)
    padded_keys = jnp.pad(key_rows, ((RADIUS, RADIUS), (0, 0), (0, 0)))
    padded_values = jnp.pad(value_rows, ((RADIUS, RADIUS), (0, 0), (0, 0)))

    def attend(block_id):
        start = block_id * block
        query_blk = lax.dynamic_slice_in_dim(query_rows, start, block, 0).astype(jnp.float32)
        key_blk = lax.dynamic_slice_in_dim(padded_keys, start, span, 0).astype(jnp.float32)
        value_blk = lax.dynamic_slice_in_dim(padded_values, start, span, 0).astype(jnp.float32)
        query_pos = start + jnp.arange(block, dtype=jnp.int32)
        key_pos = start - RADIUS + jnp.arange(span, dtype=jnp.int32)
        usable = (jnp.abs(query_pos[:, None] - key_pos[None, :]) <= RADIUS) & (key_pos[None, :] >= 0) & (key_pos[None, :] < length)
        scores = jnp.einsum('qhd,khd->hqk', query_blk, key_blk) / HD ** 0.5
        scores = jnp.where(usable[None], scores, -jnp.inf)
        top = lax.optimization_barrier(jnp.max(scores, axis=-1, keepdims=True))
        expo = jnp.exp(scores - top)
        prob_rows = (expo / lax.optimization_barrier(jnp.sum(expo, axis=-1, keepdims=True))).astype(jnp.bfloat16)
        context = jnp.einsum('hqk,khd->qhd', prob_rows.astype(jnp.float32), value_blk)
        return context.astype(jnp.bfloat16).reshape(block, D)
    context = lax.map(attend, jnp.arange(length // block, dtype=jnp.int32)).reshape(length, D)
    mixed = jnp.dot(context, attn_out, preferred_element_type=jnp.float32)
    updated = (residual.astype(jnp.float32) + mixed).astype(jnp.bfloat16)
    owned = updated.reshape(N_SEQ, TOK_SEQ, D)
    picked = jax.vmap(lambda rows_all, index_row: jnp.take(rows_all, index_row, axis=0))(owned, route_rows)
    picked = picked.reshape(N_SEQ * CAP, D)
    normed_rows = rms_norm(picked, ffn_gain)
    gate_part = jnp.dot(normed_rows, ffn_in[0], preferred_element_type=jnp.float32)
    up_part = jnp.dot(normed_rows, ffn_in[1], preferred_element_type=jnp.float32)
    hidden = (jax.nn.gelu(gate_part, approximate=True) * up_part).astype(jnp.bfloat16)
    width = FF // N_TP

    def add_group(group, total):
        start = jnp.asarray(group, jnp.int32) * width
        part_hidden = lax.dynamic_slice_in_dim(hidden, start, width, 1)
        part_weight = lax.dynamic_slice_in_dim(ffn_out, start, width, 0)
        term = jnp.dot(part_hidden, part_weight, preferred_element_type=jnp.float32).astype(jnp.bfloat16)
        term = lax.optimization_barrier(term)
        return total + term.astype(jnp.float32)
    heavy = lax.fori_loop(0, N_TP, add_group, jnp.zeros((N_SEQ * CAP, D), jnp.float32))
    slots = jnp.arange(CAP, dtype=jnp.int32)
    usable_slots = slots[None, :] < route_counts[:, None]
    heavy = jnp.where(usable_slots[:, :, None], heavy.reshape(N_SEQ, CAP, D), 0.0)
    result = jax.vmap(lambda rows_all, index_row, extra: rows_all.at[index_row].add(extra))(owned.astype(jnp.float32), route_rows, heavy)
    return result.reshape(TOKENS, D).astype(jnp.bfloat16)
```

```python
import jax
import jax.numpy as jnp
from jax import lax
from jax.experimental import pallas as pl
from jax.experimental.pallas import tpu as pltpu
from jax.sharding import PartitionSpec as P

MESH = pl.DeviceIdType.MESH
F32 = jnp.float32
BF16 = jnp.bfloat16
EPS = 1e-06
RADIUS = 127
NEG = -1e30
SIDE = 4
CHIPS = SIDE * SIDE
TOK = 2048
HALF = TOK // 2
BAND = HALF // 2
QUART = BAND // 2
LANES = 128
FEAT = CHIPS * LANES
HEADW = 64
CAP = 224
CAPC = CAP // 2
FFU = 640
HALO = 128
QBLK = 128


def gelu(v):
    return 0.5 * v * (1.0 + jnp.tanh(0.7978845608028654 * (v + 0.044715 * v * v * v)))


def kernel(
    res, wqkv, wout, ffi, ffo, gains, route, counts,
    out,
    xa, xo, wa, wb, wo, fi, fo, w2, xg, acc, ssq, qs, kv, ctx, bias, oh, oht,
    pb, rx1, rx2, upd, gp, pk, px, nrm, hid, pb2, rxc, sb, rxh, hv, om, ot,
    lsem, psend, precv, gsend, grecv, hsend, hrecv, r1send, r1recv, r2send, r2recv,
    asend, arecv, fsend, frecv, hvsend, hvrecv,
):
    z = lax.axis_index("seq")
    tp = lax.axis_index("tp")
    core = lax.rem(tp, 2)
    chip = tp // 2
    x = lax.rem(chip, SIDE)
    y = chip // SIDE
    partner = tp + 1 - 2 * core

    def wrap(v):
        return lax.rem(v + 2 * SIDE, SIDE)

    def chip_at(cx, cy):
        return wrap(cy) * SIDE + wrap(cx)

    def tp_at(cx, cy):
        return chip_at(cx, cy) * 2 + core

    def remote(src, dst, ssem, rsem, dev):
        return pltpu.make_async_remote_copy(
            src_ref=src, dst_ref=dst, send_sem=ssem, recv_sem=rsem, device_id=dev, device_id_type=MESH
        )

    def block(h, da, db):
        return chip_at(x + da, y + db) if h == 0 else chip_at(x + db, y + da)

    def near(h, axis, step):
        if (axis == 0) == (h == 0):
            return {"tp": tp_at(x + step, y)}
        return {"tp": tp_at(x, y + step)}

    SIGN = (1, -1)
    mine = pl.multiple_of(core * HALF, HALF)
    theirs = pl.multiple_of((1 - core) * HALF, HALF)

    loads = [
        pltpu.make_async_copy(res.at[pl.ds(mine, HALF)], xa, lsem.at[0]),
        pltpu.make_async_copy(wqkv, wa, lsem.at[1]),
        pltpu.make_async_copy(wout, wo.at[pl.ds(pl.multiple_of(core * HEADW, HEADW), HEADW)], lsem.at[2]),
        pltpu.make_async_copy(ffi, fi, lsem.at[3]),
        pltpu.make_async_copy(ffo, fo, lsem.at[4]),
    ]
    loads[0].start()
    loads[1].start()
    loads[2].start()

    prev_dev = {"seq": lax.rem(z + 3 + core, 4), "tp": partner}
    next_dev = {"seq": lax.rem(z + core, 4), "tp": partner}
    z_peer = {"seq": lax.rem(z + 3 + 2 * core, 4), "tp": partner}
    barrier = pltpu.get_barrier_semaphore()
    peers = [near(0, 0, 1), near(0, 0, -1), near(0, 1, 1), near(0, 1, -1), {"tp": partner}, z_peer]
    for dev in peers:
        pl.semaphore_signal(barrier, inc=1, device_id=dev, device_id_type=MESH)
    pl.semaphore_wait(barrier, len(peers))

    p_x = remote(res.at[pl.ds(theirs, HALF)], xo, psend.at[0], precv.at[0], {"tp": partner})
    p_w = remote(wqkv, wb, psend.at[1], precv.at[1], {"tp": partner})
    p_o = remote(
        wout, wo.at[pl.ds(pl.multiple_of(core * HEADW, HEADW), HEADW)], psend.at[2], precv.at[2], {"tp": partner}
    )
    p_x.start()
    p_w.start()
    p_o.start()
    loads[0].wait()
    p_x.wait_recv()
    first = core == 0
    xg[chip] = jnp.where(
        first,
        jnp.concatenate([xa[...], xo[...]], axis=1),
        jnp.concatenate([xo[...], xa[...]], axis=1),
    )

    def rows(h, part):
        base = h * BAND
        if part is None:
            return pl.ds(base, BAND)
        return pl.ds(base + part * QUART, QUART)

    def g_copy(h, item, d, index, part, axis):
        src = xg.at[index, rows(h, part)]
        return remote(src, src, gsend.at[h, item, d], grecv.at[h, item, d], near(h, axis, SIGN[d]))

    def g_item(h, item, d):
        s = SIGN[d]
        table = {
            0: (block(h, 0, 0), None, 0),
            1: (block(h, 0, 0), None, 1),
            2: (block(h, -s, 0), d, 0),
            3: (block(h, -1, 0), None, 1),
            4: (block(h, 1, 0), None, 1),
            5: (block(h, 0, -s), d, 1),
            6: (block(h, 2, 0), None, 1),
            7: (block(h, -1, -s), d, 1),
            8: (block(h, 1, -s), d, 1),
            9: (block(h, 2, -s), d, 1),
        }
        index, part, axis = table[item]
        return g_copy(h, item, d, index, part, axis)

    def g_start(item):
        for h in range(2):
            for d in range(2):
                g_item(h, item, d).start()

    def g_wait(item):
        for h in range(2):
            for d in range(2):
                g_item(h, item, d).wait_recv()

    g_start(0)
    g_start(1)
    loads[3].start()
    loads[4].start()

    loads[1].wait()
    p_w.wait_recv()

    def prep_w(k, carry):
        at = pl.ds(pl.multiple_of(k * LANES, LANES), LANES)
        r_i = lax.broadcasted_iota(jnp.int32, (LANES, LANES), 0)
        c_i = lax.broadcasted_iota(jnp.int32, (LANES, LANES), 1)
        gain_col = jnp.sum(jnp.where(r_i == c_i, gains[0, k], 0.0), axis=1, keepdims=True)
        for p in range(3):
            own = wa[p, at, :]
            oth = wb[p, at, :]
            both = jnp.where(
                first, jnp.concatenate([own, oth], axis=1), jnp.concatenate([oth, own], axis=1)
            )
            w2[k, :, p * LANES : (p + 1) * LANES] = (both.astype(F32) * gain_col).astype(BF16)
        return carry

    lax.fori_loop(0, CHIPS, prep_w, 0)

    g_wait(0)
    g_start(2)
    g_start(3)
    g_start(4)

    acc[...] = jnp.zeros_like(acc)
    ssq[...] = jnp.zeros_like(ssq)

    def qkv_pair(i1, i2):
        wpair = jnp.concatenate([w2[i1], w2[i2]], axis=0)

        def step(t, carry):
            at = pl.ds(pl.multiple_of(t * QUART, QUART), QUART)
            b1 = xg[i1, at]
            b2 = xg[i2, at]
            acc[at] += jnp.dot(jnp.concatenate([b1, b2], axis=1), wpair, preferred_element_type=F32)
            f1 = b1.astype(F32)
            f2 = b2.astype(F32)
            ssq[at] += f1 * f1 + f2 * f2
            return carry

        lax.fori_loop(0, HALF // QUART, step, 0)

    def route_tables():
        row = route[...].astype(F32)
        r_i = lax.broadcasted_iota(jnp.int32, (CAP, CAP), 0)
        c_i = lax.broadcasted_iota(jnp.int32, (CAP, CAP), 1)
        shift = (core * HALF).astype(F32)
        col = jnp.sum(jnp.where(r_i == c_i, row, 0.0), axis=1, keepdims=True) - shift
        lane = lax.broadcasted_iota(jnp.int32, (CAP, HALF), 1).astype(F32)
        oh[...] = jnp.where(lane == col, 1.0, 0.0).astype(BF16)
        sub = lax.broadcasted_iota(jnp.int32, (HALF, CAP), 0).astype(F32)
        oht[...] = jnp.where(sub == row - shift, 1.0, 0.0).astype(BF16)
        q_i = lax.broadcasted_iota(jnp.int32, (QBLK, 3 * QBLK), 0)
        k_i = lax.broadcasted_iota(jnp.int32, (QBLK, 3 * QBLK), 1) - QBLK
        band = jnp.where(jnp.abs(q_i - k_i) <= RADIUS, 0.0, NEG)
        no_prev = jnp.where(z + core == 0, NEG, 0.0)
        no_next = jnp.where(z + core == 4, NEG, 0.0)
        bias[0] = band + jnp.where(k_i < 0, no_prev, 0.0)
        bias[1] = band
        bias[2] = band + jnp.where(k_i >= QBLK, no_next, 0.0)

    route_tables()

    g_wait(1)
    g_start(5)
    qkv_pair(chip_at(x - 1, y), chip_at(x + 1, y))
    g_wait(2)
    g_start(6)
    qkv_pair(chip_at(x, y - 1), chip_at(x, y + 1))
    g_wait(3)
    g_start(7)
    g_wait(4)
    g_start(8)
    g_wait(5)
    qkv_pair(chip_at(x - 1, y - 1), chip_at(x + 1, y - 1))
    qkv_pair(chip_at(x - 1, y + 1), chip_at(x + 1, y + 1))
    g_wait(6)
    g_start(9)
    qkv_pair(chip_at(x + 2, y), chip_at(x, y + 2))
    g_wait(7)
    g_wait(8)
    qkv_pair(chip_at(x + 2, y - 1), chip_at(x + 2, y + 1))
    qkv_pair(chip_at(x - 1, y + 2), chip_at(x + 1, y + 2))
    g_wait(9)
    qkv_pair(chip, chip_at(x + 2, y + 2))

    def finish_qkv(t, carry):
        at = pl.ds(pl.multiple_of(t * QUART, QUART), QUART)
        scale = lax.rsqrt(jnp.sum(ssq[at], axis=1, keepdims=True) * (1.0 / FEAT) + EPS)
        qs[at] = (acc[at, 0:LANES] * scale).astype(BF16)
        kv[pl.ds(pl.multiple_of(HALO + t * QUART, HALO), QUART), :] = (acc[at, LANES:] * scale).astype(BF16)
        return carry

    lax.fori_loop(0, HALF // QUART, finish_qkv, 0)

    h_prev = remote(kv.at[pl.ds(HALO, HALO)], kv.at[pl.ds(HALO + HALF, HALO)], hsend.at[0], hrecv.at[0], prev_dev)
    h_next = remote(kv.at[pl.ds(HALF, HALO)], kv.at[pl.ds(0, HALO)], hsend.at[1], hrecv.at[1], next_dev)
    h_prev.start()
    h_next.start()

    low_lane = lax.broadcasted_iota(jnp.int32, (QBLK, LANES), 1) < HEADW

    def attend(i, kind):
        at = pl.ds(pl.multiple_of(i * QBLK, QBLK), QBLK)
        keys = pl.ds(pl.multiple_of(i * QBLK, QBLK), 3 * QBLK)
        q = qs[at]
        zero = jnp.zeros_like(q)
        q2 = jnp.concatenate([jnp.where(low_lane, q, zero), jnp.where(low_lane, zero, q)], axis=0)
        s = lax.dot_general(q2, kv[keys, 0:LANES], (((1,), (1,)), ((), ())), preferred_element_type=F32)
        b = bias[kind]
        s = s * (1.0 / HEADW**0.5) + jnp.concatenate([b, b], axis=0)
        top = jnp.max(s, axis=1, keepdims=True)
        e = jnp.exp(s - top)
        total = jnp.sum(e, axis=1, keepdims=True)
        o = jnp.dot(e.astype(BF16), kv[keys, LANES:], preferred_element_type=F32) / total
        ctx[at] = jnp.where(low_lane, o[:QBLK], o[QBLK:]).astype(BF16)

    def attend_mid(i, carry):
        attend(i, 1)
        return carry

    lax.fori_loop(1, HALF // QBLK - 1, attend_mid, 0)
    h_prev.wait_recv()
    h_next.wait_recv()
    attend(0, 0)
    attend(HALF // QBLK - 1, 2)

    loads[2].wait()
    p_o.wait_recv()

    def wo_cols(index):
        return wo[:, pl.ds(pl.multiple_of(index * LANES, LANES), LANES)]

    def project(step):
        for h in range(2):
            lhs = ctx[h * BAND : (h + 1) * BAND]
            for pair in ((2, -1), (1, 0)):
                i1 = block(h, pair[0], step)
                i2 = block(h, pair[1], step)
                w = jnp.concatenate([wo_cols(i1), wo_cols(i2)], axis=1)
                o = jnp.dot(lhs, w, preferred_element_type=F32).astype(BF16)
                pb[i1, rows(h, None)] = o[:, :LANES]
                pb[i2, rows(h, None)] = o[:, LANES:]

    OFF = (2, -1, 1, 0)

    def r1_copy(h, j, kind, d):
        s = SIGN[d]
        db, part = ((2, d), (s, d), (s, 1 - d))[kind]
        src = pb.at[block(h, OFF[j], db), rows(h, part)]
        return remote(
            src, rx1.at[h, j, kind, d], r1send.at[h, j, kind, d], r1recv.at[h, j, kind, d], near(h, 1, s)
        )

    def r2_copy(h, kind, d):
        s = SIGN[d]
        da, part = ((2, d), (s, d), (s, 1 - d))[kind]
        src = pb.at[block(h, da, 0), rows(h, part)]
        return remote(src, rx2.at[h, kind, d], r2send.at[h, kind, d], r2recv.at[h, kind, d], near(h, 0, s))

    both_hd = [(h, d) for h in range(2) for d in range(2)]

    def r1_start(j, kind):
        for h, d in both_hd:
            r1_copy(h, j, kind, d).start()

    def r2_start(kind):
        for h, d in both_hd:
            r2_copy(h, kind, d).start()

    def relay1(j):
        for h, d in both_hd:
            r1_copy(h, j, 0, d).wait_recv()
            s = SIGN[d]
            index = block(h, OFF[j], s)
            at = rows(h, d)
            pb[index, at] = (pb[index, at].astype(F32) + rx1[h, j, 0, d].astype(F32)).astype(BF16)
            r1_copy(h, j, 1, d).start()

    def sum1(h, j, part):
        got = pb[block(h, OFF[j], 0), rows(h, part)].astype(F32)
        return got + rx1[h, j, 1, part].astype(F32) + rx1[h, j, 2, 1 - part].astype(F32)

    def total1(j):
        for h in range(2):
            for d in range(2):
                r1_copy(h, j, 1, d).wait_recv()
                r1_copy(h, j, 2, d).wait_recv()
            for part in range(2):
                pb[block(h, OFF[j], 0), rows(h, part)] = sum1(h, j, part).astype(BF16)

    project(2)
    r1_start(0, 0)
    r1_start(1, 0)
    r1_start(2, 0)
    project(1)
    project(-1)
    r1_start(0, 2)
    relay1(0)
    r1_start(1, 2)
    r1_start(2, 2)
    r1_start(3, 0)
    project(0)
    relay1(1)
    relay1(2)
    total1(0)
    r2_start(0)
    r1_start(3, 2)
    total1(1)
    total1(2)
    r2_start(2)
    relay1(3)
    for h, d in both_hd:
        r2_copy(h, 0, d).wait_recv()
        index = block(h, SIGN[d], 0)
        at = rows(h, d)
        pb[index, at] = (pb[index, at].astype(F32) + rx2[h, 0, d].astype(F32)).astype(BF16)
        r2_copy(h, 1, d).start()
    for h in range(2):
        for d in range(2):
            r1_copy(h, 3, 1, d).wait_recv()
            r1_copy(h, 3, 2, d).wait_recv()
            r2_copy(h, 1, d).wait_recv()
            r2_copy(h, 2, d).wait_recv()
        for part in range(2):
            mixed = sum1(h, 3, part) + rx2[h, 1, part].astype(F32) + rx2[h, 2, 1 - part].astype(F32)
            at = rows(h, part)
            upd[at] = (xg[chip, at].astype(F32) + mixed).astype(BF16)

    mine_r = pl.multiple_of(core * CAPC, 16)
    theirs_r = pl.multiple_of((1 - core) * CAPC, 16)
    pk[...] = jnp.dot(oh[...], upd[...], preferred_element_type=F32).astype(BF16)
    p_pick = remote(pk.at[pl.ds(theirs_r, CAPC)], px, psend.at[3], precv.at[3], {"tp": partner})
    p_pick.start()
    p_pick.wait_recv()
    gp[chip, pl.ds(mine_r, CAPC)] = (pk[pl.ds(mine_r, CAPC)].astype(F32) + px[...].astype(F32)).astype(BF16)

    def offset(k):
        return k % SIDE, k // SIDE

    def a_copy(k):
        dx, dy = offset(k)
        src = gp.at[chip, pl.ds(mine_r, CAPC)]
        return remote(src, src, asend.at[k], arecv.at[k], {"tp": tp_at(x + dx, y + dy)})

    def f_copy(k):
        dx, dy = offset(k)
        src = gp.at[chip_at(x - dx, y - dy), pl.ds(mine_r, CAPC)]
        return remote(src, src, fsend.at[k], frecv.at[k], {"tp": partner})

    order = [10, 2, 8, 6, 9, 11, 14, 5, 7, 13, 15, 1, 3, 4, 12]
    for k in order:
        a_copy(k).start()
    f_copy(0).start()
    for k in reversed(order):
        a_copy(k).wait_recv()
        f_copy(k).start()
    for k in range(CHIPS):
        f_copy(k).wait_recv()

    sq = jnp.zeros((CAP, LANES), F32)
    for k in range(CHIPS):
        v = gp[k].astype(F32)
        sq = sq + v * v
    scale = lax.rsqrt(jnp.sum(sq, axis=1, keepdims=True) * (1.0 / FEAT) + EPS)
    for k in range(CHIPS):
        nrm[:, k * LANES : (k + 1) * LANES] = (gp[k].astype(F32) * scale * gains[1, k]).astype(BF16)

    loads[3].wait()
    for n0, nw in ((0, 256), (256, 256), (512, 128)):
        rows_n = nrm[...]
        gate = jnp.dot(rows_n, fi[0, :, n0 : n0 + nw], preferred_element_type=F32)
        up = jnp.dot(rows_n, fi[1, :, n0 : n0 + nw], preferred_element_type=F32)
        hid[:, n0 : n0 + nw] = (gelu(gate) * up).astype(BF16)
    loads[4].wait()
    for n in range(CHIPS // 2):
        o = jnp.dot(hid[...], fo[:, n * 256 : (n + 1) * 256], preferred_element_type=F32).astype(BF16)
        pb2[2 * n] = o[:, :LANES]
        pb2[2 * n + 1] = o[:, LANES:]

    p_part = remote(pb2.at[:, pl.ds(theirs_r, CAPC)], rxc, psend.at[4], precv.at[4], {"tp": partner})
    p_part.start()
    p_part.wait_recv()
    for k in range(CHIPS):
        sb[k] = (pb2[k, pl.ds(mine_r, CAPC)].astype(F32) + rxc[k].astype(F32)).astype(BF16)

    def hv_copy(k):
        dx, dy = offset(k)
        return remote(
            sb.at[chip_at(x + dx, y + dy)], rxh.at[k], hvsend.at[k], hvrecv.at[k], {"tp": tp_at(x + dx, y + dy)}
        )

    for k in order:
        hv_copy(k).start()
    heavy = sb[chip].astype(F32)
    for k in reversed(order):
        hv_copy(k).wait_recv()
        heavy = heavy + rxh[k].astype(F32)
    slot = lax.broadcasted_iota(jnp.int32, (CAPC, LANES), 0) + core * CAPC
    heavy = jnp.where(slot < counts[z], heavy, 0.0)
    high = heavy.astype(BF16)
    hv[pl.ds(mine_r, CAPC), 0:LANES] = high
    hv[pl.ds(mine_r, CAPC), LANES:] = (heavy - high.astype(F32)).astype(BF16)
    hv_part = hv.at[pl.ds(mine_r, CAPC)]
    p_hv = remote(hv_part, hv_part, psend.at[5], precv.at[5], {"tp": partner})
    p_hv.start()
    p_hv.wait_recv()

    added = jnp.dot(oht[...], hv[...], preferred_element_type=F32)
    final = (upd[...].astype(F32) + added[:, :LANES] + added[:, LANES:]).astype(BF16)
    om[...] = jnp.where(first, final[:, :HEADW], final[:, HEADW:])
    ot[...] = jnp.where(first, final[:, HEADW:], final[:, :HEADW])
    out_part = out.at[pl.ds(mine, HALF)]
    p_out = remote(ot, out_part, psend.at[6], precv.at[6], {"tp": partner})
    p_out.start()
    l_out = pltpu.make_async_copy(om, out_part, lsem.at[5])
    l_out.start()

    for h, d in both_hd:
        for item in range(10):
            g_item(h, item, d).wait_send()
        for j in range(4):
            for kind in range(3):
                r1_copy(h, j, kind, d).wait_send()
        for kind in range(3):
            r2_copy(h, kind, d).wait_send()
    for copy in (p_x, p_w, p_o, h_prev, h_next, p_pick, p_part, p_hv):
        copy.wait_send()
    f_copy(0).wait_send()
    for k in order:
        a_copy(k).wait_send()
        f_copy(k).wait_send()
        hv_copy(k).wait_send()
    l_out.wait()
    p_out.wait()


def local(
    residual, attn_gain, attn_in, attn_out, ffn_gain, ffn_in, ffn_out, route_rows, route_counts
):
    gains = jnp.stack([attn_gain, ffn_gain]).astype(F32).reshape(2, CHIPS, 1, LANES)
    any_spec = pl.BlockSpec(memory_space=pl.ANY)
    vm = pltpu.VMEM
    dma = pltpu.SemaphoreType.DMA
    return pl.pallas_call(
        kernel,
        out_shape=jax.ShapeDtypeStruct((TOK, HEADW), BF16),
        in_specs=[any_spec] * 5
        + [pl.BlockSpec(memory_space=pltpu.VMEM)] * 2
        + [pl.BlockSpec(memory_space=pltpu.SMEM)],
        out_specs=any_spec,
        scratch_shapes=[
            vm((HALF, HEADW), BF16),
            vm((HALF, HEADW), BF16),
            vm((3, FEAT, HEADW), BF16),
            vm((3, FEAT, HEADW), BF16),
            vm((LANES, FEAT), BF16),
            vm((2, FEAT, FFU), BF16),
            vm((FFU, FEAT), BF16),
            vm((CHIPS, LANES, 3 * LANES), BF16),
            vm((CHIPS, HALF, LANES), BF16),
            vm((HALF, 3 * LANES), F32),
            vm((HALF, LANES), F32),
            vm((HALF, LANES), BF16),
            vm((HALF + 2 * HALO, 2 * LANES), BF16),
            vm((HALF, LANES), BF16),
            vm((3, QBLK, 3 * QBLK), F32),
            vm((CAP, HALF), BF16),
            vm((HALF, CAP), BF16),
            vm((CHIPS, HALF, LANES), BF16),
            vm((2, 4, 3, 2, QUART, LANES), BF16),
            vm((2, 3, 2, QUART, LANES), BF16),
            vm((HALF, LANES), BF16),
            vm((CHIPS, CAP, LANES), BF16),
            vm((CAP, LANES), BF16),
            vm((CAPC, LANES), BF16),
            vm((CAP, FEAT), BF16),
            vm((CAP, FFU), BF16),
            vm((CHIPS, CAP, LANES), BF16),
            vm((CHIPS, CAPC, LANES), BF16),
            vm((CHIPS, CAPC, LANES), BF16),
            vm((CHIPS, CAPC, LANES), BF16),
            vm((CAP, 2 * LANES), BF16),
            vm((HALF, HEADW), BF16),
            vm((HALF, HEADW), BF16),
            dma((6,)),
            dma((7,)),
            dma((7,)),
            dma((2, 10, 2)),
            dma((2, 10, 2)),
            dma((2,)),
            dma((2,)),
            dma((2, 4, 3, 2)),
            dma((2, 4, 3, 2)),
            dma((2, 3, 2)),
            dma((2, 3, 2)),
            dma((CHIPS,)),
            dma((CHIPS,)),
            dma((CHIPS,)),
            dma((CHIPS,)),
            dma((CHIPS,)),
            dma((CHIPS,)),
        ],
        compiler_params=pltpu.CompilerParams(
            collective_id=0, has_side_effects=True, vmem_limit_bytes=62 * 1024 * 1024
        ),
        name="layer",
    )(residual, attn_in, attn_out, ffn_in, ffn_out, gains, route_rows, route_counts)


def solution(mesh):
    in_specs = (
        P("seq", "tp"),
        P(),
        P(None, None, "tp"),
        P("tp", None),
        P(),
        P(None, None, "tp"),
        P("tp", None),
        P("seq", None),
        P(),
    )
    out_specs = P("seq", "tp")
    return jax.shard_map(local, mesh=mesh, in_specs=in_specs, out_specs=out_specs, check_vma=False)
```

```python
import jax
import jax.numpy as jnp
from jax import lax
from jax.experimental import pallas as pl
from jax.experimental.pallas import tpu as pltpu
from jax.sharding import PartitionSpec as P

MESH = pl.DeviceIdType.MESH
F32 = jnp.float32
BF16 = jnp.bfloat16
EPS = 1e-06
RADIUS = 127
NEG = -1e30
SIDE = 4
CHIPS = SIDE * SIDE
TOK = 2048
HALF = TOK // 2
QUART = HALF // 4
LANES = 128
FEAT = CHIPS * LANES
HEADW = 64
CAP = 224
CAPC = CAP // 2
FFU = 640
QBLK = 128
NBLK = HALF // QBLK
OFF = (2, -1, 1, 0)
SIGN = (1, -1)


def gelu(v):
    return 0.5 * v * (1.0 + jnp.tanh(0.7978845608028654 * (v + 0.044715 * v * v * v)))


def dot(a, b):
    return jnp.dot(a, b, preferred_element_type=F32)


def dot_nt(a, b):
    return lax.dot_general(a, b, (((1,), (1,)), ((), ())), preferred_element_type=F32)


def dot_tn(a, b):
    return lax.dot_general(a, b, (((0,), (0,)), ((), ())), preferred_element_type=F32)


def kernel(
    res, wqkv, wout, ffi, ffo, gain_a, gain_f, route, counts,
    out,
    wraw, wo, wot, fi, fo, w2, xg, acc, ssq, qt, kvb, ctx, bias, oh,
    pb, rx1, rx2, upd, fin, gp, pk, px, nrm, hid, pb2, rxc, sb, rxa, sb2, rxb, hv,
    lsem, xlsem, xsend, xrecv, psend, precv, gsend, grecv, hsend, hrecv,
    r1send, r1recv, r2send, r2recv, s1send, s1recv, s2send, s2recv,
    asend, arecv, fsend, frecv, csend, crecv,
):
    z = lax.axis_index("seq")
    tp = lax.axis_index("tp")
    core = lax.rem(tp, 2)
    chip = tp // 2
    x = lax.rem(chip, SIDE)
    y = chip // SIDE
    partner = {"tp": tp + 1 - 2 * core}

    def wrap(v):
        return lax.rem(v + 2 * SIDE, SIDE)

    def chip_at(cx, cy):
        return wrap(cy) * SIDE + wrap(cx)

    def tp_at(cx, cy):
        return chip_at(cx, cy) * 2 + core

    flights = {}

    class Flight:
        def __init__(self, key, copy):
            self.key, self.copy = key, copy

        def start(self):
            flights[self.key] = [self.copy, False]
            self.copy.start()

        def wait_recv(self):
            flights[self.key][1] = True
            self.copy.wait_recv()

    def remote(key, src, dst, ssem, rsem, dev):
        copy = pltpu.make_async_remote_copy(
            src_ref=src, dst_ref=dst, send_sem=ssem, recv_sem=rsem, device_id=dev, device_id_type=MESH
        )
        return Flight(key, copy)

    def settle():
        for copy, seen in flights.values():
            if not seen:
                copy.wait_recv()
            copy.wait_send()

    def block(h, da, db):
        return chip_at(x + da, y + db) if h == 0 else chip_at(x + db, y + da)

    def near(h, axis, step):
        if (axis == 0) == (h == 0):
            return {"tp": tp_at(x + step, y)}
        return {"tp": tp_at(x, y + step)}

    def small_block(da, db):
        return chip_at(x + da + core * (db - da), y + db + core * (da - db))

    def small_near(da, db):
        return {"tp": small_block(da, db) * 2 + core}

    first = core == 0
    own_feat = pl.ds(pl.multiple_of(core * HEADW, HEADW), HEADW)
    oth_feat = pl.ds(pl.multiple_of((1 - core) * HEADW, HEADW), HEADW)

    def tokens(half, q):
        return pl.ds(pl.multiple_of(half * HALF + q * QUART, QUART), QUART)

    def w_rows(p):
        return pl.ds(pl.multiple_of(p * LANES + core * HEADW, HEADW), HEADW)

    load_x = [
        pltpu.make_async_copy(res.at[:, tokens(core, q)], xg.at[chip, q, own_feat], xlsem.at[q]) for q in range(4)
    ]
    load_w = [pltpu.make_async_copy(wqkv.at[p], wraw.at[w_rows(p)], xlsem.at[4 + p]) for p in range(3)]
    load_o = pltpu.make_async_copy(wout, wo.at[own_feat], lsem.at[0])
    load_fi = pltpu.make_async_copy(ffi, fi, lsem.at[1])
    load_fo = pltpu.make_async_copy(ffo, fo, lsem.at[2])
    for copy in load_x + load_w:
        copy.start()
    load_o.start()

    other = tp + 1 - 2 * core
    prev_dev = {"seq": lax.rem(z + 3 + core, 4), "tp": other}
    next_dev = {"seq": lax.rem(z + core, 4), "tp": other}
    z_peer = {"seq": lax.rem(z + 3 + 2 * core, 4), "tp": other}
    barrier = pltpu.get_barrier_semaphore()
    peers = [near(0, 0, 1), near(0, 0, -1), near(0, 1, 1), near(0, 1, -1), partner, z_peer]
    for dev in peers:
        pl.semaphore_signal(barrier, inc=1, device_id=dev, device_id_type=MESH)
    pl.semaphore_wait(barrier, len(peers))

    swap_x = [
        remote(("x", q), res.at[:, tokens(1 - core, q)], xg.at[chip, q, own_feat], xsend.at[q], xrecv.at[q], partner)
        for q in range(4)
    ]
    swap_w = [
        remote(("w", p), wqkv.at[p], wraw.at[w_rows(p)], xsend.at[4 + p], xrecv.at[4 + p], partner) for p in range(3)
    ]
    swap_o = remote("o", wout, wo.at[own_feat], psend.at[0], precv.at[0], partner)
    for copy in swap_x + swap_w:
        copy.start()
    swap_o.start()

    def quarters(h, part):
        return pl.ds(2 * h, 2) if part is None else pl.ds(2 * h + part, 1)

    def g_item(h, item, d):
        s = SIGN[d]
        index, part, axis = {
            0: (block(h, 0, 0), None, 0),
            1: (block(h, 0, 0), None, 1),
            2: (block(h, -s, 0), d, 0),
            3: (block(h, -1, 0), None, 1),
            4: (block(h, 1, 0), None, 1),
            5: (block(h, 0, -s), d, 1),
            6: (block(h, 2, 0), None, 1),
            7: (block(h, -1, -s), d, 1),
            8: (block(h, 1, -s), d, 1),
            9: (block(h, 2, -s), d, 1),
        }[item]
        src = xg.at[index, quarters(h, part)]
        return remote(("g", h, item, d), src, src, gsend.at[h, item, d], grecv.at[h, item, d], near(h, axis, s))

    both_hd = [(h, d) for h in range(2) for d in range(2)]

    def g_start(item):
        for h, d in both_hd:
            g_item(h, item, d).start()

    def g_wait(item):
        for h, d in both_hd:
            g_item(h, item, d).wait_recv()

    for h in range(2):
        for q in (2 * h, 2 * h + 1):
            load_x[q].wait()
            swap_x[q].wait_recv()
        for d in range(2):
            g_item(h, 0, d).start()
    g_start(1)
    load_fi.start()
    load_fo.start()

    for p in range(3):
        load_w[p].wait()
        swap_w[p].wait_recv()
    for k in range(CHIPS):
        cols = slice(k * LANES, (k + 1) * LANES)
        w2[k] = (wraw[:, cols].astype(F32) * gain_a[cols].astype(F32).reshape(1, LANES)).astype(BF16)

    g_wait(0)
    g_start(2)
    g_start(3)
    g_start(4)

    acc[...] = jnp.zeros_like(acc)
    ssq[...] = jnp.zeros_like(ssq)

    def qkv_pair(i1, i2):
        wpair = jnp.concatenate([w2[i1], w2[i2]], axis=1)

        def step(q, carry):
            xx = jnp.concatenate([xg[i1, q], xg[i2, q]], axis=0)
            acc[q] += dot(wpair, xx)
            f = xx.astype(F32)
            ssq[q] += jnp.sum((f * f).reshape(2 * LANES // 8, 8, QUART), axis=0)
            return carry

        lax.fori_loop(0, 4, step, 0)

    row = route[...].astype(F32)
    r_i = lax.broadcasted_iota(jnp.int32, (CAP, CAP), 0)
    c_i = lax.broadcasted_iota(jnp.int32, (CAP, CAP), 1)
    col = jnp.sum(jnp.where(r_i == c_i, row, 0.0), axis=1, keepdims=True) - (core * HALF).astype(F32)
    lane = lax.broadcasted_iota(jnp.int32, (CAP, HALF), 1).astype(F32)
    oh[...] = jnp.where(lane == col, 1.0, 0.0).astype(BF16)
    k_i = lax.broadcasted_iota(jnp.int32, (3 * QBLK, QBLK), 0) - QBLK
    q_i = lax.broadcasted_iota(jnp.int32, (3 * QBLK, QBLK), 1)
    band = jnp.where(jnp.abs(q_i - k_i) <= RADIUS, 0.0, NEG)
    bias[0] = band + jnp.where(k_i < 0, jnp.where(z + core == 0, NEG, 0.0), 0.0)
    bias[1] = band
    bias[2] = band + jnp.where(k_i >= QBLK, jnp.where(z + core == 4, NEG, 0.0), 0.0)
    load_o.wait()
    swap_o.wait_recv()
    for k in range(CHIPS):
        at = slice(k * LANES, (k + 1) * LANES)
        wot[at] = wo[:, at].astype(F32).T.astype(BF16)

    g_wait(1)
    g_start(5)
    qkv_pair(chip_at(x - 1, y), chip_at(x + 1, y))
    g_wait(2)
    g_start(6)
    qkv_pair(chip_at(x, y - 1), chip_at(x, y + 1))
    g_wait(3)
    g_start(7)
    g_wait(4)
    g_start(8)

    mine_r = pl.ds(pl.multiple_of(core * CAPC, 16), CAPC)
    theirs_r = pl.ds(pl.multiple_of((1 - core) * CAPC, 16), CAPC)

    def pick(block_of):
        total = jnp.zeros((CAP, LANES), F32)
        for q in range(4):
            total = total + dot_nt(oh[:, q * QUART : (q + 1) * QUART], block_of(q))
        return total.astype(BF16)

    pk[0] = pick(lambda q: xg[chip, q])
    swap_r = [
        remote(("r", i), pk.at[i, theirs_r], px.at[i], psend.at[1 + i], precv.at[1 + i], partner) for i in range(2)
    ]
    swap_r[0].start()

    g_wait(5)
    qkv_pair(chip_at(x - 1, y - 1), chip_at(x + 1, y - 1))
    qkv_pair(chip_at(x - 1, y + 1), chip_at(x + 1, y + 1))
    g_wait(6)
    g_start(9)
    qkv_pair(chip_at(x + 2, y), chip_at(x, y + 2))
    g_wait(7)
    g_wait(8)
    qkv_pair(chip_at(x + 2, y - 1), chip_at(x + 2, y + 1))
    qkv_pair(chip_at(x - 1, y + 2), chip_at(x + 1, y + 2))
    g_wait(9)
    qkv_pair(chip, chip_at(x + 2, y + 2))

    def finish_qkv(q):
        scale = lax.rsqrt(jnp.sum(ssq[q], axis=0, keepdims=True) * (1.0 / FEAT) + EPS)
        qt[:, q * QUART : (q + 1) * QUART] = (
            (acc[q, 0:LANES] * scale).astype(BF16).astype(F32) * (1.0 / HEADW**0.5)
        ).astype(BF16)
        keys = (acc[q, LANES : 2 * LANES] * scale).T.astype(BF16)
        vals = (acc[q, 2 * LANES :] * scale).astype(BF16)
        for half in range(2):
            at = slice(half * QBLK, (half + 1) * QBLK)
            kvb[1 + 2 * q + half, 0] = keys[at]
            kvb[1 + 2 * q + half, 1] = vals[:, at]

    h_prev = remote("hp", kvb.at[1], kvb.at[NBLK + 1], hsend.at[0], hrecv.at[0], prev_dev)
    h_next = remote("hn", kvb.at[NBLK], kvb.at[0], hsend.at[1], hrecv.at[1], next_dev)
    finish_qkv(0)
    finish_qkv(3)
    h_prev.start()
    h_next.start()
    finish_qkv(1)
    finish_qkv(2)

    def attend(i, kind):
        at = pl.ds(pl.multiple_of(i * QBLK, QBLK), QBLK)
        q = qt[:, at]
        zero = jnp.zeros((HEADW, QBLK), BF16)
        q2 = jnp.concatenate(
            [jnp.concatenate([q[:HEADW], zero], axis=0), jnp.concatenate([zero, q[HEADW:]], axis=0)], axis=1
        )
        keys = jnp.concatenate([kvb[i, 0], kvb[i + 1, 0], kvb[i + 2, 0]], axis=0)
        vals = jnp.concatenate([kvb[i, 1], kvb[i + 1, 1], kvb[i + 2, 1]], axis=1)
        b = bias[kind]
        s = dot(keys, q2) + jnp.concatenate([b, b], axis=1)
        e = jnp.exp(s - jnp.max(s, axis=0, keepdims=True))
        total = jnp.sum(e, axis=0, keepdims=True)
        o = dot(vals, e.astype(BF16)) / total
        ctx[:, at] = jnp.concatenate([o[:HEADW, :QBLK], o[HEADW:, QBLK:]], axis=0).astype(BF16)

    def attend_mid(i, carry):
        attend(i, 1)
        return carry

    lax.fori_loop(1, NBLK - 1, attend_mid, 0)
    h_prev.wait_recv()
    h_next.wait_recv()
    attend(0, 0)
    attend(NBLK - 1, 2)

    def wot_rows(index):
        return wot[pl.ds(pl.multiple_of(index * LANES, LANES), LANES), :]

    def project(step):
        for h in range(2):
            rhs = ctx[:, 2 * h * QUART : 2 * (h + 1) * QUART]
            for pair in ((2, -1), (1, 0)):
                i1 = block(h, pair[0], step)
                i2 = block(h, pair[1], step)
                o = dot(jnp.concatenate([wot_rows(i1), wot_rows(i2)], axis=0), rhs).astype(BF16)
                for part in range(2):
                    at = slice(part * QUART, (part + 1) * QUART)
                    pb[i1, 2 * h + part] = o[:LANES, at]
                    pb[i2, 2 * h + part] = o[LANES:, at]

    def r1_copy(h, j, kind, d):
        s = SIGN[d]
        db, part = ((2, d), (s, d), (s, 1 - d))[kind]
        src = pb.at[block(h, OFF[j], db), 2 * h + part]
        return remote(
            ("r1", h, j, kind, d), src, rx1.at[h, j, kind, d], r1send.at[h, j, kind, d], r1recv.at[h, j, kind, d], near(h, 1, s)
        )

    def r2_copy(h, kind, d):
        s = SIGN[d]
        da, part = ((2, d), (s, d), (s, 1 - d))[kind]
        src = pb.at[block(h, da, 0), 2 * h + part]
        return remote(("r2", h, kind, d), src, rx2.at[h, kind, d], r2send.at[h, kind, d], r2recv.at[h, kind, d], near(h, 0, s))

    def r1_start(j, kind):
        for h, d in both_hd:
            r1_copy(h, j, kind, d).start()

    def r2_start(kind):
        for h, d in both_hd:
            r2_copy(h, kind, d).start()

    def relay1(j):
        for h, d in both_hd:
            r1_copy(h, j, 0, d).wait_recv()
            index = block(h, OFF[j], SIGN[d])
            q = 2 * h + d
            pb[index, q] = (pb[index, q].astype(F32) + rx1[h, j, 0, d].astype(F32)).astype(BF16)
            r1_copy(h, j, 1, d).start()

    def relay2():
        for h, d in both_hd:
            r2_copy(h, 0, d).wait_recv()
            index = block(h, SIGN[d], 0)
            q = 2 * h + d
            pb[index, q] = (pb[index, q].astype(F32) + rx2[h, 0, d].astype(F32)).astype(BF16)
            r2_copy(h, 1, d).start()

    def sum1(h, j, part):
        got = pb[block(h, OFF[j], 0), 2 * h + part].astype(F32)
        return got + rx1[h, j, 1, part].astype(F32) + rx1[h, j, 2, 1 - part].astype(F32)

    def wait1(h, j):
        for d in range(2):
            r1_copy(h, j, 1, d).wait_recv()
            r1_copy(h, j, 2, d).wait_recv()

    def total1(j):
        for h in range(2):
            wait1(h, j)
            for part in range(2):
                pb[block(h, OFF[j], 0), 2 * h + part] = sum1(h, j, part).astype(BF16)

    def last():
        for h in range(2):
            wait1(h, 3)
            for d in range(2):
                r2_copy(h, 1, d).wait_recv()
                r2_copy(h, 2, d).wait_recv()
            for part in range(2):
                mixed = sum1(h, 3, part) + rx2[h, 1, part].astype(F32) + rx2[h, 2, 1 - part].astype(F32)
                q = 2 * h + part
                upd[q] = (xg[chip, q].astype(F32) + mixed).astype(BF16)

    def s1_copy(n, t, j):
        src = sb.at[n, small_block(t, j)]
        return remote(("s1", n, t, j), src, rxa.at[n, t - 1, j], s1send.at[n, t - 1, j], s1recv.at[n, t - 1, j], small_near(t, 0))

    def s2_copy(n, t):
        src = sb2.at[n, t]
        return remote(("s2", n, t), src, rxb.at[n, t - 1], s2send.at[n, t - 1], s2recv.at[n, t - 1], small_near(0, t))

    STEPS = (2, 1, 3)
    COLS = (2, 1, 3, 0)

    def small_start(n):
        for j in COLS:
            for t in STEPS:
                s1_copy(n, t, j).start()

    def small_mid(n):
        for j in COLS:
            total = sb[n, small_block(0, j)].astype(F32)
            for t in STEPS:
                s1_copy(n, t, j).wait_recv()
                total = total + rxa[n, t - 1, j].astype(F32)
            sb2[n, j] = total.astype(BF16)
            if j > 0:
                s2_copy(n, j).start()

    def small_end(n):
        total = sb2[n, 0].astype(F32)
        for t in STEPS:
            s2_copy(n, t).wait_recv()
            total = total + rxb[n, t - 1].astype(F32)
        return total

    def a_copy(t, j):
        if t == 0:
            src = gp.at[chip, mine_r]
            return remote(("a", 0, j), src, src, asend.at[0, j], arecv.at[0, j], small_near(0, j))
        src = gp.at[small_block(0, -j), mine_r]
        return remote(("a", t, j), src, src, asend.at[t, j], arecv.at[t, j], small_near(t, 0))

    def f_copy(t, j):
        src = gp.at[small_block(-t, -j), mine_r]
        return remote(("f", t, j), src, src, fsend.at[t, j], frecv.at[t, j], partner)

    def gather_first():
        for j in STEPS:
            a_copy(0, j).start()
        for t in STEPS:
            a_copy(t, 0).start()
        f_copy(0, 0).start()

    def gather_second():
        for j in (1, 3, 2):
            a_copy(0, j).wait_recv()
            for t in STEPS:
                a_copy(t, j).start()
            f_copy(0, j).start()

    def gather_third():
        for j in (0, 1, 3, 2):
            for t in (1, 3, 2):
                a_copy(t, j).wait_recv()
                f_copy(t, j).start()

    def gather_last():
        for j in range(SIDE):
            for t in range(SIDE):
                f_copy(t, j).wait_recv()

    pk[1] = pick(lambda q: ctx[:, q * QUART : (q + 1) * QUART])
    swap_r[1].start()
    project(2)
    r1_start(0, 0)
    swap_r[0].wait_recv()
    swap_r[1].wait_recv()
    rows_ctx = (pk[1, mine_r].astype(F32) + px[1].astype(F32)).astype(BF16)
    for k in range(CHIPS // 2):
        o = dot(rows_ctx, wo[:, k * 256 : (k + 1) * 256]).astype(BF16)
        sb[0, 2 * k] = o[:, :LANES]
        sb[0, 2 * k + 1] = o[:, LANES:]
    small_start(0)
    project(1)
    project(-1)
    r1_start(0, 2)
    small_mid(0)
    r1_start(1, 0)
    relay1(0)
    rows_new = pk[0, mine_r].astype(F32) + px[0].astype(F32) + small_end(0)
    gp[chip, mine_r] = rows_new.astype(BF16)
    gather_first()
    r1_start(2, 0)
    project(0)
    gather_second()
    r1_start(1, 2)
    relay1(1)
    gather_third()
    r1_start(2, 2)
    r1_start(3, 0)
    relay1(2)
    total1(0)
    r2_start(0)
    gather_last()

    sq = jnp.zeros((CAP, LANES), F32)
    for k in range(CHIPS):
        v = gp[k].astype(F32)
        sq = sq + v * v
    scale = lax.rsqrt(jnp.sum(sq, axis=1, keepdims=True) * (1.0 / FEAT) + EPS)
    for k in range(CHIPS):
        at = slice(k * LANES, (k + 1) * LANES)
        nrm[:, at] = (gp[k].astype(F32) * scale * gain_f[at].astype(F32).reshape(1, LANES)).astype(BF16)

    r1_start(3, 2)
    load_fi.wait()

    def ffn_in(n0, nw):
        rows_n = nrm[...]
        gate = dot(rows_n, fi[0, :, n0 : n0 + nw])
        up = dot(rows_n, fi[1, :, n0 : n0 + nw])
        hid[:, n0 : n0 + nw] = (gelu(gate) * up).astype(BF16)

    ffn_in(0, 256)
    total1(1)
    total1(2)
    r2_start(2)
    ffn_in(256, 256)
    relay1(3)
    ffn_in(512, 128)
    relay2()
    load_fo.wait()

    def c_copy(n):
        pair = pl.ds(2 * n, 2)
        return remote(("c", n), pb2.at[pair, theirs_r], rxc.at[pair], csend.at[n], crecv.at[n], partner)

    for n in range(CHIPS // 2):
        o = dot(hid[...], fo[:, n * 256 : (n + 1) * 256]).astype(BF16)
        pb2[2 * n] = o[:, :LANES]
        pb2[2 * n + 1] = o[:, LANES:]
        c_copy(n).start()
    for n in range(CHIPS // 2):
        c_copy(n).wait_recv()
        for k in (2 * n, 2 * n + 1):
            sb[1, k] = (pb2[k, mine_r].astype(F32) + rxc[k].astype(F32)).astype(BF16)
    small_start(1)
    last()
    small_mid(1)
    heavy = small_end(1)
    slot = lax.broadcasted_iota(jnp.int32, (CAPC, LANES), 0) + core * CAPC
    heavy = jnp.where(slot < counts[z], heavy, 0.0)
    high = heavy.astype(BF16)
    hv[mine_r, 0:LANES] = high
    hv[mine_r, LANES:] = (heavy - high.astype(F32)).astype(BF16)
    swap_h = remote("h", hv.at[mine_r], hv.at[mine_r], psend.at[3], precv.at[3], partner)
    swap_h.start()
    swap_h.wait_recv()

    for q in range(4):
        at = slice(q * QUART, (q + 1) * QUART)
        added = dot_tn(hv[...], oh[:, at])
        fin[:, at] = (upd[q].astype(F32) + added[:LANES] + added[LANES:]).astype(BF16)
    out_part = out.at[:, pl.ds(pl.multiple_of(core * HALF, HALF), HALF)]
    send_out = remote("out", fin.at[oth_feat], out_part, psend.at[4], precv.at[4], partner)
    send_out.start()
    save_out = pltpu.make_async_copy(fin.at[own_feat], out_part, lsem.at[3])
    save_out.start()

    save_out.wait()
    settle()


def local(
    residual, attn_gain, attn_in, attn_out, ffn_gain, ffn_in, ffn_out, route_rows, route_counts
):
    any_spec = pl.BlockSpec(memory_space=pl.ANY)
    vm = pltpu.VMEM
    dma = pltpu.SemaphoreType.DMA
    turned = pl.pallas_call(
        kernel,
        out_shape=jax.ShapeDtypeStruct((HEADW, TOK), BF16),
        in_specs=[any_spec] * 5
        + [pl.BlockSpec(memory_space=pltpu.VMEM)] * 3
        + [pl.BlockSpec(memory_space=pltpu.SMEM)],
        out_specs=any_spec,
        scratch_shapes=[
            vm((3 * LANES, FEAT), BF16),
            vm((LANES, FEAT), BF16),
            vm((FEAT, LANES), BF16),
            vm((2, FEAT, FFU), BF16),
            vm((FFU, FEAT), BF16),
            vm((CHIPS, 3 * LANES, LANES), BF16),
            vm((CHIPS, 4, LANES, QUART), BF16),
            vm((4, 3 * LANES, QUART), F32),
            vm((4, 8, QUART), F32),
            vm((LANES, HALF), BF16),
            vm((NBLK + 2, 2, QBLK, QBLK), BF16),
            vm((LANES, HALF), BF16),
            vm((3, 3 * QBLK, QBLK), F32),
            vm((CAP, HALF), BF16),
            vm((CHIPS, 4, LANES, QUART), BF16),
            vm((2, 4, 3, 2, LANES, QUART), BF16),
            vm((2, 3, 2, LANES, QUART), BF16),
            vm((4, LANES, QUART), BF16),
            vm((LANES, HALF), BF16),
            vm((CHIPS, CAP, LANES), BF16),
            vm((2, CAP, LANES), BF16),
            vm((2, CAPC, LANES), BF16),
            vm((CAP, FEAT), BF16),
            vm((CAP, FFU), BF16),
            vm((CHIPS, CAP, LANES), BF16),
            vm((CHIPS, CAPC, LANES), BF16),
            vm((2, CHIPS, CAPC, LANES), BF16),
            vm((2, 3, SIDE, CAPC, LANES), BF16),
            vm((2, SIDE, CAPC, LANES), BF16),
            vm((2, 3, CAPC, LANES), BF16),
            vm((CAP, 2 * LANES), BF16),
            dma((4,)),
            dma((7,)),
            dma((7,)),
            dma((7,)),
            dma((5,)),
            dma((5,)),
            dma((2, 10, 2)),
            dma((2, 10, 2)),
            dma((2,)),
            dma((2,)),
            dma((2, 4, 3, 2)),
            dma((2, 4, 3, 2)),
            dma((2, 3, 2)),
            dma((2, 3, 2)),
            dma((2, 3, SIDE)),
            dma((2, 3, SIDE)),
            dma((2, 3)),
            dma((2, 3)),
            dma((SIDE, SIDE)),
            dma((SIDE, SIDE)),
            dma((SIDE, SIDE)),
            dma((SIDE, SIDE)),
            dma((CHIPS // 2,)),
            dma((CHIPS // 2,)),
        ],
        compiler_params=pltpu.CompilerParams(
            collective_id=0, has_side_effects=True, vmem_limit_bytes=62 * 1024 * 1024
        ),
        name="layer",
    )(
        residual.T, attn_in.transpose(0, 2, 1), attn_out, ffn_in, ffn_out, attn_gain, ffn_gain, route_rows, route_counts
    )
    return turned.T


def solution(mesh):
    in_specs = (
        P("seq", "tp"),
        P(),
        P(None, None, "tp"),
        P("tp", None),
        P(),
        P(None, None, "tp"),
        P("tp", None),
        P("seq", None),
        P(),
    )
    out_specs = P("seq", "tp")
    return jax.shard_map(local, mesh=mesh, in_specs=in_specs, out_specs=out_specs, check_vma=False)
```

```python
import jax
import jax.numpy as jnp
from jax import lax
from jax.experimental import pallas as pl
from jax.experimental.pallas import tpu as pltpu
from jax.sharding import PartitionSpec as P

MESH = pl.DeviceIdType.MESH
F32 = jnp.float32
BF16 = jnp.bfloat16
EPS = 1e-06
RADIUS = 127
NEG = -1e30
SIDE = 4
CHIPS = SIDE * SIDE
TOK = 2048
HALF = TOK // 2
QUART = HALF // 4
LANES = 128
FEAT = CHIPS * LANES
HEADW = 64
CAP = 224
CAPC = CAP // 2
FFU = 640
QBLK = 128
NBLK = HALF // QBLK
OFF = (2, -1, 1, 0)
SIGN = (1, -1)


def gelu(v):
    return 0.5 * v * (1.0 + jnp.tanh(0.7978845608028654 * (v + 0.044715 * v * v * v)))


def dot(a, b):
    return jnp.dot(a, b, preferred_element_type=F32)


def dot_nt(a, b):
    return lax.dot_general(a, b, (((1,), (1,)), ((), ())), preferred_element_type=F32)


def dot_tn(a, b):
    return lax.dot_general(a, b, (((0,), (0,)), ((), ())), preferred_element_type=F32)


def kernel(
    res, wqkv, wout, ffi, ffo, gain_a, gain_f, route, counts,
    out,
    wraw, wo, wot, fi, fo, w2, xg, acc, ssq, qt, kvb, ctx, bias, oh,
    pb, rx1, rx2, upd, fin, gp, pk, px, nrm, hid, pb2, rxc, sb, rxa, sb2, rxb, hv,
    loads, sends, recvs, grecv, rrecv, s1recv, s2recv, arecv, crecv,
):
    z = lax.axis_index("seq")
    tp = lax.axis_index("tp")
    core = lax.rem(tp, 2)
    chip = tp // 2
    x = lax.rem(chip, SIDE)
    y = chip // SIDE
    partner = {"tp": tp + 1 - 2 * core}

    def wrap(v):
        return lax.rem(v + 2 * SIDE, SIDE)

    def chip_at(cx, cy):
        return wrap(cy) * SIDE + wrap(cx)

    def tp_at(cx, cy):
        return chip_at(cx, cy) * 2 + core

    def remote(src, dst, ssem, rsem, dev):
        return pltpu.make_async_remote_copy(
            src_ref=src, dst_ref=dst, send_sem=ssem, recv_sem=rsem, device_id=dev, device_id_type=MESH
        )

    def arrived(sem, ref):
        remote(ref, ref, sends.at[0], sem, partner).wait_recv()

    def left(n, ref):
        remote(ref, ref, sends.at[n], recvs.at[0], partner).wait_send()

    def block(h, da, db):
        return chip_at(x + da, y + db) if h == 0 else chip_at(x + db, y + da)

    def near(h, axis, step):
        if (axis == 0) == (h == 0):
            return {"tp": tp_at(x + step, y)}
        return {"tp": tp_at(x, y + step)}

    def small_block(da, db):
        return chip_at(x + da + core * (db - da), y + db + core * (da - db))

    def small_near(da, db):
        return {"tp": small_block(da, db) * 2 + core}

    first = core == 0
    own_feat = pl.ds(pl.multiple_of(core * HEADW, HEADW), HEADW)
    oth_feat = pl.ds(pl.multiple_of((1 - core) * HEADW, HEADW), HEADW)

    def tokens(half, q):
        return pl.ds(pl.multiple_of(half * HALF + q * QUART, QUART), QUART)

    def w_rows(p):
        return pl.ds(pl.multiple_of(p * LANES + core * HEADW, HEADW), HEADW)

    load_x = [
        pltpu.make_async_copy(res.at[:, tokens(core, q)], xg.at[chip, q, own_feat], loads.at[0]) for q in range(4)
    ]
    load_w = [pltpu.make_async_copy(wqkv.at[p], wraw.at[w_rows(p)], loads.at[1]) for p in range(3)]
    load_o = pltpu.make_async_copy(wout, wo.at[own_feat], loads.at[2])
    load_fi = pltpu.make_async_copy(ffi, fi, loads.at[3])
    load_fo = pltpu.make_async_copy(ffo, fo, loads.at[4])
    for copy in load_x + load_w:
        copy.start()
    load_o.start()

    other = tp + 1 - 2 * core
    prev_dev = {"seq": lax.rem(z + 3 + core, 4), "tp": other}
    next_dev = {"seq": lax.rem(z + core, 4), "tp": other}
    z_peer = {"seq": lax.rem(z + 3 + 2 * core, 4), "tp": other}
    barrier = pltpu.get_barrier_semaphore()
    peers = [near(0, 0, 1), near(0, 0, -1), near(0, 1, 1), near(0, 1, -1), partner, z_peer]
    for dev in peers:
        pl.semaphore_signal(barrier, inc=1, device_id=dev, device_id_type=MESH)
    pl.semaphore_wait(barrier, len(peers))

    swap_x = [
        remote(res.at[:, tokens(1 - core, q)], xg.at[chip, q, own_feat], sends.at[0], recvs.at[q // 2], partner)
        for q in range(4)
    ]
    swap_w = [
        remote(wqkv.at[p], wraw.at[w_rows(p)], sends.at[1], recvs.at[2], partner) for p in range(3)
    ]
    swap_o = remote(wout, wo.at[own_feat], sends.at[2], recvs.at[3], partner)
    for copy in swap_x + swap_w:
        copy.start()
    swap_o.start()

    def quarters(h, part):
        return pl.ds(2 * h, 2) if part is None else pl.ds(2 * h + part, 1)

    def g_item(h, item, d, piece=None):
        s = SIGN[d]
        index, part, axis = {
            0: (block(h, 0, 0), None, 0),
            1: (block(h, 0, 0), None, 1),
            2: (block(h, -s, 0), d, 0),
            3: (block(h, -1, 0), None, 1),
            4: (block(h, 1, 0), None, 1),
            5: (block(h, 0, -s), d, 1),
            6: (block(h, 2, 0), None, 1),
            7: (block(h, -1, -s), d, 1),
            8: (block(h, 1, -s), d, 1),
            9: (block(h, 2, -s), d, 1),
        }[item]
        feats = {None: pl.ds(0, LANES), 0: own_feat, 1: oth_feat}[piece]
        src = xg.at[index, quarters(h, part), feats]
        return remote(src, src, sends.at[3], grecv.at[item], near(h, axis, s))

    both_hd = [(h, d) for h in range(2) for d in range(2)]

    def g_start(item):
        for h, d in both_hd:
            g_item(h, item, d).start()

    def g_wait(item):
        arrived(grecv.at[item], xg.at[0:2] if item in (0, 1, 3, 4, 6) else xg.at[0])

    pltpu.make_async_copy(xg.at[0, 0:2], xg.at[0, 0:2], loads.at[0]).wait()
    for item in range(2):
        for h, d in both_hd:
            g_item(h, item, d, 0).start()
    for h in range(2):
        arrived(recvs.at[h], xg.at[0, 0])
        for d in range(2):
            g_item(h, 0, d, 1).start()
    for h, d in both_hd:
        g_item(h, 1, d, 1).start()
    load_fi.start()
    load_fo.start()

    pltpu.make_async_copy(wraw.at[0 : 3 * HEADW], wraw.at[0 : 3 * HEADW], loads.at[1]).wait()
    arrived(recvs.at[2], wraw.at[0 : 3 * HEADW])
    for k in range(CHIPS):
        cols = slice(k * LANES, (k + 1) * LANES)
        w2[k] = (wraw[:, cols].astype(F32) * gain_a[cols].astype(F32).reshape(1, LANES)).astype(BF16)

    g_wait(0)
    g_start(2)
    g_start(3)
    g_start(4)

    acc[...] = jnp.zeros_like(acc)
    ssq[...] = jnp.zeros_like(ssq)

    def qkv_pair(i1, i2):
        wpair = jnp.concatenate([w2[i1], w2[i2]], axis=1)

        def step(q, carry):
            xx = jnp.concatenate([xg[i1, q], xg[i2, q]], axis=0)
            acc[q] += dot(wpair, xx)
            f = xx.astype(F32)
            ssq[q] += jnp.sum((f * f).reshape(2 * LANES // 8, 8, QUART), axis=0)
            return carry

        lax.fori_loop(0, 4, step, 0)

    row = route[...].astype(F32)
    r_i = lax.broadcasted_iota(jnp.int32, (CAP, CAP), 0)
    c_i = lax.broadcasted_iota(jnp.int32, (CAP, CAP), 1)
    col = jnp.sum(jnp.where(r_i == c_i, row, 0.0), axis=1, keepdims=True) - (core * HALF).astype(F32)
    lane = lax.broadcasted_iota(jnp.int32, (CAP, HALF), 1).astype(F32)
    oh[...] = jnp.where(lane == col, 1.0, 0.0).astype(BF16)
    k_i = lax.broadcasted_iota(jnp.int32, (3 * QBLK, QBLK), 0) - QBLK
    q_i = lax.broadcasted_iota(jnp.int32, (3 * QBLK, QBLK), 1)
    band = jnp.where(jnp.abs(q_i - k_i) <= RADIUS, 0.0, NEG)
    bias[0] = band + jnp.where(k_i < 0, jnp.where(z + core == 0, NEG, 0.0), 0.0)
    bias[1] = band
    bias[2] = band + jnp.where(k_i >= QBLK, jnp.where(z + core == 4, NEG, 0.0), 0.0)
    load_o.wait()
    arrived(recvs.at[3], wo.at[0:HEADW])
    for k in range(CHIPS):
        at = slice(k * LANES, (k + 1) * LANES)
        wot[at] = wo[:, at].astype(F32).T.astype(BF16)

    g_wait(1)
    g_start(5)
    qkv_pair(chip_at(x - 1, y), chip_at(x + 1, y))
    g_wait(2)
    g_start(6)
    qkv_pair(chip_at(x, y - 1), chip_at(x, y + 1))
    g_wait(3)
    g_start(7)
    g_wait(4)
    g_start(8)

    mine_r = pl.ds(pl.multiple_of(core * CAPC, 16), CAPC)
    theirs_r = pl.ds(pl.multiple_of((1 - core) * CAPC, 16), CAPC)

    def pick(block_of):
        total = jnp.zeros((CAP, LANES), F32)
        for q in range(4):
            total = total + dot_nt(oh[:, q * QUART : (q + 1) * QUART], block_of(q))
        return total.astype(BF16)

    pk[0] = pick(lambda q: xg[chip, q])
    swap_r = [
        remote(pk.at[i, theirs_r], px.at[i], sends.at[4], recvs.at[4 + i], partner) for i in range(2)
    ]
    swap_r[0].start()

    g_wait(5)
    qkv_pair(chip_at(x - 1, y - 1), chip_at(x + 1, y - 1))
    qkv_pair(chip_at(x - 1, y + 1), chip_at(x + 1, y + 1))
    g_wait(6)
    g_start(9)
    qkv_pair(chip_at(x + 2, y), chip_at(x, y + 2))
    g_wait(7)
    g_wait(8)
    qkv_pair(chip_at(x + 2, y - 1), chip_at(x + 2, y + 1))
    qkv_pair(chip_at(x - 1, y + 2), chip_at(x + 1, y + 2))
    g_wait(9)
    qkv_pair(chip, chip_at(x + 2, y + 2))

    def finish_qkv(q):
        scale = lax.rsqrt(jnp.sum(ssq[q], axis=0, keepdims=True) * (1.0 / FEAT) + EPS)
        qt[:, q * QUART : (q + 1) * QUART] = (
            (acc[q, 0:LANES] * scale).astype(BF16).astype(F32) * (1.0 / HEADW**0.5)
        ).astype(BF16)
        keys = (acc[q, LANES : 2 * LANES] * scale).T.astype(BF16)
        vals = (acc[q, 2 * LANES :] * scale).astype(BF16)
        for half in range(2):
            at = slice(half * QBLK, (half + 1) * QBLK)
            kvb[1 + 2 * q + half, 0] = keys[at]
            kvb[1 + 2 * q + half, 1] = vals[:, at]

    h_prev = remote(kvb.at[1], kvb.at[NBLK + 1], sends.at[5], recvs.at[6], prev_dev)
    h_next = remote(kvb.at[NBLK], kvb.at[0], sends.at[5], recvs.at[7], next_dev)
    finish_qkv(0)
    finish_qkv(3)
    h_prev.start()
    h_next.start()
    finish_qkv(1)
    finish_qkv(2)

    def attend(i, kind):
        at = pl.ds(pl.multiple_of(i * QBLK, QBLK), QBLK)
        q = qt[:, at]
        zero = jnp.zeros((HEADW, QBLK), BF16)
        q2 = jnp.concatenate(
            [jnp.concatenate([q[:HEADW], zero], axis=0), jnp.concatenate([zero, q[HEADW:]], axis=0)], axis=1
        )
        keys = jnp.concatenate([kvb[i, 0], kvb[i + 1, 0], kvb[i + 2, 0]], axis=0)
        vals = jnp.concatenate([kvb[i, 1], kvb[i + 1, 1], kvb[i + 2, 1]], axis=1)
        b = bias[kind]
        s = dot(keys, q2) + jnp.concatenate([b, b], axis=1)
        e = jnp.exp(s - jnp.max(s, axis=0, keepdims=True))
        total = jnp.sum(e, axis=0, keepdims=True)
        o = dot(vals, e.astype(BF16)) / total
        ctx[:, at] = jnp.concatenate([o[:HEADW, :QBLK], o[HEADW:, QBLK:]], axis=0).astype(BF16)

    def attend_mid(i, carry):
        attend(i, 1)
        return carry

    lax.fori_loop(1, NBLK - 1, attend_mid, 0)
    arrived(recvs.at[6], kvb.at[0])
    arrived(recvs.at[7], kvb.at[0])
    attend(0, 0)
    attend(NBLK - 1, 2)

    def wot_rows(index):
        return wot[pl.ds(pl.multiple_of(index * LANES, LANES), LANES), :]

    def project(step):
        for h in range(2):
            rhs = ctx[:, 2 * h * QUART : 2 * (h + 1) * QUART]
            for pair in ((2, -1), (1, 0)):
                i1 = block(h, pair[0], step)
                i2 = block(h, pair[1], step)
                o = dot(jnp.concatenate([wot_rows(i1), wot_rows(i2)], axis=0), rhs).astype(BF16)
                for part in range(2):
                    at = slice(part * QUART, (part + 1) * QUART)
                    pb[i1, 2 * h + part] = o[:LANES, at]
                    pb[i2, 2 * h + part] = o[LANES:, at]

    def r1_copy(h, j, kind, d):
        s = SIGN[d]
        db, part = ((2, d), (s, d), (s, 1 - d))[kind]
        src = pb.at[block(h, OFF[j], db), 2 * h + part]
        return remote(src, rx1.at[h, j, kind, d], sends.at[6], rrecv.at[j if kind == 0 else 4 + j], near(h, 1, s))

    def r2_copy(h, kind, d):
        s = SIGN[d]
        da, part = ((2, d), (s, d), (s, 1 - d))[kind]
        src = pb.at[block(h, da, 0), 2 * h + part]
        return remote(src, rx2.at[h, kind, d], sends.at[6], rrecv.at[8 if kind == 0 else 9], near(h, 0, s))

    def r1_start(j, kind):
        for h, d in both_hd:
            r1_copy(h, j, kind, d).start()

    def r2_start(kind):
        for h, d in both_hd:
            r2_copy(h, kind, d).start()

    def relay1(j):
        arrived(rrecv.at[j], xg.at[0])
        for h, d in both_hd:
            index = block(h, OFF[j], SIGN[d])
            q = 2 * h + d
            pb[index, q] = (pb[index, q].astype(F32) + rx1[h, j, 0, d].astype(F32)).astype(BF16)
            r1_copy(h, j, 1, d).start()

    def relay2():
        arrived(rrecv.at[8], xg.at[0])
        for h, d in both_hd:
            index = block(h, SIGN[d], 0)
            q = 2 * h + d
            pb[index, q] = (pb[index, q].astype(F32) + rx2[h, 0, d].astype(F32)).astype(BF16)
            r2_copy(h, 1, d).start()

    def sum1(h, j, part):
        got = pb[block(h, OFF[j], 0), 2 * h + part].astype(F32)
        return got + rx1[h, j, 1, part].astype(F32) + rx1[h, j, 2, 1 - part].astype(F32)

    def total1(j):
        arrived(rrecv.at[4 + j], xg.at[0:2])
        for h in range(2):
            for part in range(2):
                pb[block(h, OFF[j], 0), 2 * h + part] = sum1(h, j, part).astype(BF16)

    def last():
        arrived(rrecv.at[7], xg.at[0:2])
        arrived(rrecv.at[9], xg.at[0:2])
        for h in range(2):
            for part in range(2):
                mixed = sum1(h, 3, part) + rx2[h, 1, part].astype(F32) + rx2[h, 2, 1 - part].astype(F32)
                q = 2 * h + part
                upd[q] = (xg[chip, q].astype(F32) + mixed).astype(BF16)

    def s1_copy(n, t, j):
        src = sb.at[n, small_block(t, j)]
        return remote(src, rxa.at[n, t - 1, j], sends.at[7], s1recv.at[n, j], small_near(t, 0))

    def s2_copy(n, t):
        src = sb2.at[n, t]
        return remote(src, rxb.at[n, t - 1], sends.at[7], s2recv.at[n], small_near(0, t))

    STEPS = (2, 1, 3)
    COLS = (2, 1, 3, 0)

    def small_start(n):
        for j in COLS:
            for t in STEPS:
                s1_copy(n, t, j).start()

    def small_mid(n):
        for j in COLS:
            total = sb[n, small_block(0, j)].astype(F32)
            arrived(s1recv.at[n, j], sb.at[n, 0:3])
            for t in STEPS:
                total = total + rxa[n, t - 1, j].astype(F32)
            sb2[n, j] = total.astype(BF16)
            if j > 0:
                s2_copy(n, j).start()

    def small_end(n):
        total = sb2[n, 0].astype(F32)
        arrived(s2recv.at[n], sb.at[n, 0:3])
        for t in STEPS:
            total = total + rxb[n, t - 1].astype(F32)
        return total

    def a_copy(t, j):
        if t == 0:
            src = gp.at[chip, mine_r]
            return remote(src, src, sends.at[8], arecv.at[3 + j], small_near(0, j))
        src = gp.at[small_block(0, -j), mine_r]
        return remote(src, src, sends.at[8], arecv.at[j], small_near(t, 0))

    def f_copy(t, j):
        src = gp.at[small_block(-t, -j), mine_r]
        return remote(src, src, sends.at[9], recvs.at[8], partner)

    def gather_first():
        for j in STEPS:
            a_copy(0, j).start()
        for t in STEPS:
            a_copy(t, 0).start()
        f_copy(0, 0).start()

    def gather_second():
        for j in (1, 3, 2):
            arrived(arecv.at[3 + j], sb.at[0, 0])
            for t in STEPS:
                a_copy(t, j).start()
            f_copy(0, j).start()

    def gather_third():
        for j in (0, 1, 3, 2):
            arrived(arecv.at[j], sb.at[0, 0:3])
            for t in (1, 3, 2):
                f_copy(t, j).start()

    def gather_last():
        arrived(recvs.at[8], sb.at[0])

    pk[1] = pick(lambda q: ctx[:, q * QUART : (q + 1) * QUART])
    swap_r[1].start()
    project(2)
    r1_start(0, 0)
    arrived(recvs.at[4], px.at[0])
    arrived(recvs.at[5], px.at[0])
    rows_ctx = (pk[1, mine_r].astype(F32) + px[1].astype(F32)).astype(BF16)
    for k in range(CHIPS // 2):
        o = dot(rows_ctx, wo[:, k * 256 : (k + 1) * 256]).astype(BF16)
        sb[0, 2 * k] = o[:, :LANES]
        sb[0, 2 * k + 1] = o[:, LANES:]
    small_start(0)
    project(1)
    project(-1)
    r1_start(0, 2)
    small_mid(0)
    r1_start(1, 0)
    relay1(0)
    rows_new = pk[0, mine_r].astype(F32) + px[0].astype(F32) + small_end(0)
    gp[chip, mine_r] = rows_new.astype(BF16)
    gather_first()
    r1_start(2, 0)
    project(0)
    gather_second()
    r1_start(1, 2)
    relay1(1)
    gather_third()
    r1_start(2, 2)
    r1_start(3, 0)
    relay1(2)
    total1(0)
    r2_start(0)
    gather_last()

    sq = jnp.zeros((CAP, LANES), F32)
    for k in range(CHIPS):
        v = gp[k].astype(F32)
        sq = sq + v * v
    scale = lax.rsqrt(jnp.sum(sq, axis=1, keepdims=True) * (1.0 / FEAT) + EPS)
    for k in range(CHIPS):
        at = slice(k * LANES, (k + 1) * LANES)
        nrm[:, at] = (gp[k].astype(F32) * scale * gain_f[at].astype(F32).reshape(1, LANES)).astype(BF16)

    r1_start(3, 2)
    load_fi.wait()

    def ffn_in(n0, nw):
        rows_n = nrm[...]
        gate = dot(rows_n, fi[0, :, n0 : n0 + nw])
        up = dot(rows_n, fi[1, :, n0 : n0 + nw])
        hid[:, n0 : n0 + nw] = (gelu(gate) * up).astype(BF16)

    ffn_in(0, 256)
    total1(1)
    total1(2)
    r2_start(2)
    ffn_in(256, 256)
    relay1(3)
    ffn_in(512, 128)
    relay2()
    load_fo.wait()

    def c_copy(n):
        pair = pl.ds(2 * n, 2)
        return remote(pb2.at[pair, theirs_r], rxc.at[pair], sends.at[10], crecv.at[n // 2], partner)

    for n in range(CHIPS // 2):
        o = dot(hid[...], fo[:, n * 256 : (n + 1) * 256]).astype(BF16)
        pb2[2 * n] = o[:, :LANES]
        pb2[2 * n + 1] = o[:, LANES:]
        c_copy(n).start()
    for n in range(4):
        arrived(crecv.at[n], sb.at[0, 0:4])
        for k in range(4 * n, 4 * n + 4):
            sb[1, k] = (pb2[k, mine_r].astype(F32) + rxc[k].astype(F32)).astype(BF16)
    small_start(1)
    last()
    small_mid(1)
    heavy = small_end(1)
    slot = lax.broadcasted_iota(jnp.int32, (CAPC, LANES), 0) + core * CAPC
    heavy = jnp.where(slot < counts[z], heavy, 0.0)
    high = heavy.astype(BF16)
    hv[mine_r, 0:LANES] = high
    hv[mine_r, LANES:] = (heavy - high.astype(F32)).astype(BF16)
    swap_h = remote(hv.at[mine_r], hv.at[mine_r], sends.at[11], recvs.at[9], partner)
    swap_h.start()
    arrived(recvs.at[9], hv.at[0:CAPC])

    for q in range(4):
        at = slice(q * QUART, (q + 1) * QUART)
        added = dot_tn(hv[...], oh[:, at])
        fin[:, at] = (upd[q].astype(F32) + added[:LANES] + added[LANES:]).astype(BF16)
    out_part = out.at[:, pl.ds(pl.multiple_of(core * HALF, HALF), HALF)]
    send_out = remote(fin.at[oth_feat], out_part, sends.at[12], recvs.at[10], partner)
    send_out.start()
    save_out = pltpu.make_async_copy(fin.at[own_feat], out_part, loads.at[5])
    save_out.start()

    left(0, xg.at[0, 0:2])
    left(1, wraw.at[0 : 3 * HEADW])
    left(2, wo.at[0:HEADW])
    left(3, xg.at[0:15])
    left(4, px)
    left(5, kvb.at[0:2])
    left(6, pb.at[0:15])
    left(7, sb.at[:, 0:15])
    left(8, sb.at[0, 0:15])
    left(9, sb.at[0])
    left(10, sb.at[1])
    left(11, hv.at[0:CAPC])
    save_out.wait()
    send_out.wait()


def local(
    residual, attn_gain, attn_in, attn_out, ffn_gain, ffn_in, ffn_out, route_rows, route_counts
):
    any_spec = pl.BlockSpec(memory_space=pl.ANY)
    vm = pltpu.VMEM
    dma = pltpu.SemaphoreType.DMA
    turned = pl.pallas_call(
        kernel,
        out_shape=jax.ShapeDtypeStruct((HEADW, TOK), BF16),
        in_specs=[any_spec] * 5
        + [pl.BlockSpec(memory_space=pltpu.VMEM)] * 3
        + [pl.BlockSpec(memory_space=pltpu.SMEM)],
        out_specs=any_spec,
        scratch_shapes=[
            vm((3 * LANES, FEAT), BF16),
            vm((LANES, FEAT), BF16),
            vm((FEAT, LANES), BF16),
            vm((2, FEAT, FFU), BF16),
            vm((FFU, FEAT), BF16),
            vm((CHIPS, 3 * LANES, LANES), BF16),
            vm((CHIPS, 4, LANES, QUART), BF16),
            vm((4, 3 * LANES, QUART), F32),
            vm((4, 8, QUART), F32),
            vm((LANES, HALF), BF16),
            vm((NBLK + 2, 2, QBLK, QBLK), BF16),
            vm((LANES, HALF), BF16),
            vm((3, 3 * QBLK, QBLK), F32),
            vm((CAP, HALF), BF16),
            vm((CHIPS, 4, LANES, QUART), BF16),
            vm((2, 4, 3, 2, LANES, QUART), BF16),
            vm((2, 3, 2, LANES, QUART), BF16),
            vm((4, LANES, QUART), BF16),
            vm((LANES, HALF), BF16),
            vm((CHIPS, CAP, LANES), BF16),
            vm((2, CAP, LANES), BF16),
            vm((2, CAPC, LANES), BF16),
            vm((CAP, FEAT), BF16),
            vm((CAP, FFU), BF16),
            vm((CHIPS, CAP, LANES), BF16),
            vm((CHIPS, CAPC, LANES), BF16),
            vm((2, CHIPS, CAPC, LANES), BF16),
            vm((2, 3, SIDE, CAPC, LANES), BF16),
            vm((2, SIDE, CAPC, LANES), BF16),
            vm((2, 3, CAPC, LANES), BF16),
            vm((CAP, 2 * LANES), BF16),
            dma((6,)),
            dma((13,)),
            dma((11,)),
            dma((10,)),
            dma((10,)),
            dma((2, SIDE)),
            dma((2,)),
            dma((7,)),
            dma((4,)),
        ],
        compiler_params=pltpu.CompilerParams(
            collective_id=0, has_side_effects=True, vmem_limit_bytes=62 * 1024 * 1024
        ),
        name="layer",
    )(
        residual.T, attn_in.transpose(0, 2, 1), attn_out, ffn_in, ffn_out, attn_gain, ffn_gain, route_rows, route_counts
    )
    return turned.T


def solution(mesh):
    in_specs = (
        P("seq", "tp"),
        P(),
        P(None, None, "tp"),
        P("tp", None),
        P(),
        P(None, None, "tp"),
        P("tp", None),
        P("seq", None),
        P(),
    )
    out_specs = P("seq", "tp")
    return jax.shard_map(local, mesh=mesh, in_specs=in_specs, out_specs=out_specs, check_vma=False)
```

```python
import jax
import jax.numpy as jnp
from jax import lax
from jax.experimental import pallas as pl
from jax.experimental.pallas import tpu as pltpu
from jax.sharding import PartitionSpec as P

MESH = pl.DeviceIdType.MESH
F32 = jnp.float32
BF16 = jnp.bfloat16
EPS = 1e-06
RADIUS = 127
NEG = -1e30
SIDE = 4
CHIPS = SIDE * SIDE
TOK = 2048
HALF = TOK // 2
QUART = HALF // 4
LANES = 128
FEAT = CHIPS * LANES
HEADW = 64
CAP = 224
CAPC = CAP // 2
FFU = 640
QBLK = 128
NBLK = HALF // QBLK
OFF = (2, -1, 1, 0)
SIGN = (1, -1)
CHUNK = (((0, 3), (5, 3)), ((3, 1), (4, 1)))
PAIRS = ((0, 1), (6, 7), (2, 5), (3, 4))
SETS = ((0, 3), (1, 2))


def gelu(v):
    return 0.5 * v * (1.0 + jnp.tanh(0.7978845608028654 * (v + 0.044715 * v * v * v)))


def dot(a, b):
    return jnp.dot(a, b, preferred_element_type=F32)


def dot_nt(a, b):
    return lax.dot_general(a, b, (((1,), (1,)), ((), ())), preferred_element_type=F32)


def dot_tn(a, b):
    return lax.dot_general(a, b, (((0,), (0,)), ((), ())), preferred_element_type=F32)


def kernel(
    res, wqkv, wout, ffi, ffo, gain_a, gain_f, route, counts,
    out,
    wraw, wo, wot, fi, fo, w2, xg, acc, ssq, qt, kvb, ctx, bias, oh,
    pb, rx1, rx2, upd, fin, gp, pk, px, nrm, hid, pb2, rxc, sb, rxa, sb2, rxb, rxo, hv,
    loads, sends, recvs, grecv, rrecv, s1recv, s2recv, arecv, crecv,
):
    z = lax.axis_index("seq")
    tp = lax.axis_index("tp")
    core = lax.rem(tp, 2)
    chip = tp // 2
    x = lax.rem(chip, SIDE)
    y = chip // SIDE
    partner = {"tp": tp + 1 - 2 * core}

    def wrap(v):
        return lax.rem(v + 2 * SIDE, SIDE)

    def chip_at(cx, cy):
        return wrap(cy) * SIDE + wrap(cx)

    def tp_at(cx, cy):
        return chip_at(cx, cy) * 2 + core

    def remote(src, dst, ssem, rsem, dev):
        return pltpu.make_async_remote_copy(
            src_ref=src, dst_ref=dst, send_sem=ssem, recv_sem=rsem, device_id=dev, device_id_type=MESH
        )

    def arrived(sem, ref):
        remote(ref, ref, sends.at[0], sem, partner).wait_recv()

    def left(n, ref):
        remote(ref, ref, sends.at[n], recvs.at[0], partner).wait_send()

    def block(h, da, db):
        return chip_at(x + da, y + db) if h == 0 else chip_at(x + db, y + da)

    def near(h, axis, step):
        if (axis == 0) == (h == 0):
            return {"tp": tp_at(x + step, y)}
        return {"tp": tp_at(x, y + step)}

    def small_block(da, db):
        return chip_at(x + da + core * (db - da), y + db + core * (da - db))

    def small_near(da, db):
        return {"tp": small_block(da, db) * 2 + core}

    first = core == 0
    own_feat = pl.ds(pl.multiple_of(core * HEADW, HEADW), HEADW)
    oth_feat = pl.ds(pl.multiple_of((1 - core) * HEADW, HEADW), HEADW)

    def tokens(half, b):
        return pl.ds(pl.multiple_of(half * HALF + b * QBLK, QBLK), QBLK)

    ORDER = (0, 1, 2, 5, 6, 7, 3, 4)

    def w_rows(p):
        return pl.ds(pl.multiple_of(p * LANES + core * HEADW, HEADW), HEADW)

    load_x = [
        pltpu.make_async_copy(res.at[:, tokens(core, b)], xg.at[chip, b, own_feat], loads.at[0]) for b in ORDER
    ]
    load_w = [pltpu.make_async_copy(wqkv.at[p], wraw.at[w_rows(p)], loads.at[1]) for p in range(3)]
    load_o = pltpu.make_async_copy(wout, wo.at[own_feat], loads.at[2])
    load_fi = pltpu.make_async_copy(ffi, fi, loads.at[3])
    load_fo = pltpu.make_async_copy(ffo, fo, loads.at[4])
    for copy in load_x + load_w:
        copy.start()
    load_o.start()

    other = tp + 1 - 2 * core
    prev_dev = {"seq": lax.rem(z + 3 + core, 4), "tp": other}
    next_dev = {"seq": lax.rem(z + core, 4), "tp": other}
    z_peer = {"seq": lax.rem(z + 3 + 2 * core, 4), "tp": other}
    barrier = pltpu.get_barrier_semaphore()
    peers = [near(0, 0, 1), near(0, 0, -1), near(0, 1, 1), near(0, 1, -1), partner, z_peer]
    for dev in peers:
        pl.semaphore_signal(barrier, inc=1, device_id=dev, device_id_type=MESH)
    pl.semaphore_wait(barrier, len(peers))

    swap_x = [
        remote(
            res.at[:, tokens(1 - core, b)], xg.at[chip, b, own_feat], sends.at[0],
            recvs.at[1 if b in (3, 4) else 0], partner,
        )
        for b in ORDER
    ]
    swap_w = [
        remote(wqkv.at[p], wraw.at[w_rows(p)], sends.at[1], recvs.at[2], partner) for p in range(3)
    ]
    swap_o = remote(wout, wo.at[own_feat], sends.at[2], recvs.at[3], partner)
    for copy in swap_x + swap_w:
        copy.start()
    swap_o.start()

    def g_item(c, h, item, d, piece=None):
        s = SIGN[d]
        index, part, axis = {
            0: (block(h, 0, 0), None, 0),
            1: (block(h, 0, 0), None, 1),
            2: (block(h, -s, 0), d, 0),
            3: (block(h, -1, 0), None, 1),
            4: (block(h, 1, 0), None, 1),
            5: (block(h, 0, -s), d, 1),
            6: (block(h, 2, 0), None, 1),
            7: (block(h, -1, -s), d, 1),
            8: (block(h, 1, -s), d, 1),
            9: (block(h, 2, -s), d, 1),
        }[item]
        feats = pl.ds(0, LANES) if part is None else pl.ds(part * HEADW, HEADW)
        if piece is not None:
            feats = (own_feat, oth_feat)[piece]
        start, count = CHUNK[c][h]
        src = xg.at[index, pl.ds(start, count), feats]
        return remote(src, src, sends.at[3], grecv.at[c, item], near(h, axis, s))

    both_hd = [(h, d) for h in range(2) for d in range(2)]

    def g_start(c, item, piece=None):
        for h, d in both_hd:
            g_item(c, h, item, d, piece).start()

    def g_wait(c, item):
        count = CHUNK[c][0][1] * 2
        if item in (0, 1, 3, 4, 6):
            arrived(grecv.at[c, item], xg.at[0:2, 0:count])
        else:
            arrived(grecv.at[c, item], xg.at[0, 0:count])

    pltpu.make_async_copy(xg.at[0, 0:4], xg.at[0, 0:4], loads.at[0]).wait()
    g_start(0, 0, 0)
    g_start(0, 1, 0)
    arrived(recvs.at[0], xg.at[0, 0:3])
    g_start(0, 0, 1)
    g_start(0, 1, 1)
    arrived(recvs.at[1], xg.at[0, 0])
    load_fi.start()
    load_fo.start()

    pltpu.make_async_copy(wraw.at[0 : 3 * HEADW], wraw.at[0 : 3 * HEADW], loads.at[1]).wait()
    arrived(recvs.at[2], wraw.at[0 : 3 * HEADW])
    for k in range(CHIPS):
        cols = slice(k * LANES, (k + 1) * LANES)
        w2[k] = (wraw[:, cols].astype(F32) * gain_a[cols].astype(F32).reshape(1, LANES)).astype(BF16)

    g_wait(0, 0)
    g_start(0, 2)
    g_start(0, 3)
    g_start(0, 4)

    acc[...] = jnp.zeros_like(acc)
    ssq[...] = jnp.zeros_like(ssq)

    def qkv_pair(i1, i2, pairs):
        wpair = jnp.concatenate([w2[i1], w2[i2]], axis=1)
        for u in pairs:
            b1, b2 = PAIRS[u]
            x1 = jnp.concatenate([xg[i1, b1], xg[i1, b2]], axis=1)
            x2 = jnp.concatenate([xg[i2, b1], xg[i2, b2]], axis=1)
            xx = jnp.concatenate([x1, x2], axis=0)
            acc[u] += dot(wpair, xx)
            f = xx.astype(F32)
            ssq[u] += jnp.sum((f * f).reshape(2 * LANES // 8, 8, QUART), axis=0)

    def group0(pairs):
        qkv_pair(chip_at(x - 1, y), chip_at(x + 1, y), pairs)
        qkv_pair(chip_at(x, y - 1), chip_at(x, y + 1), pairs)

    def group1(pairs):
        qkv_pair(chip_at(x - 1, y - 1), chip_at(x + 1, y - 1), pairs)
        qkv_pair(chip_at(x - 1, y + 1), chip_at(x + 1, y + 1), pairs)
        qkv_pair(chip_at(x + 2, y), chip_at(x, y + 2), pairs)

    def group2(pairs):
        qkv_pair(chip_at(x + 2, y - 1), chip_at(x + 2, y + 1), pairs)
        qkv_pair(chip_at(x - 1, y + 2), chip_at(x + 1, y + 2), pairs)

    def group3(pairs):
        qkv_pair(chip, chip_at(x + 2, y + 2), pairs)

    EARLY = (0, 1, 2)
    LATE = (3,)

    row = route[...].astype(F32)
    r_i = lax.broadcasted_iota(jnp.int32, (CAP, CAP), 0)
    c_i = lax.broadcasted_iota(jnp.int32, (CAP, CAP), 1)
    col = jnp.sum(jnp.where(r_i == c_i, row, 0.0), axis=1, keepdims=True) - (core * HALF).astype(F32)
    lane = lax.broadcasted_iota(jnp.int32, (CAP, HALF), 1).astype(F32)
    oh[...] = jnp.where(lane == col, 1.0, 0.0).astype(BF16)
    k_i = lax.broadcasted_iota(jnp.int32, (3 * QBLK, QBLK), 0) - QBLK
    q_i = lax.broadcasted_iota(jnp.int32, (3 * QBLK, QBLK), 1)
    band = jnp.where(jnp.abs(q_i - k_i) <= RADIUS, 0.0, NEG)
    bias[0] = band + jnp.where(k_i < 0, jnp.where(z + core == 0, NEG, 0.0), 0.0)
    bias[1] = band
    bias[2] = band + jnp.where(k_i >= QBLK, jnp.where(z + core == 4, NEG, 0.0), 0.0)
    load_o.wait()
    arrived(recvs.at[3], wo.at[0:HEADW])
    for k in range(CHIPS):
        at = slice(k * LANES, (k + 1) * LANES)
        wot[at] = wo[:, at].astype(F32).T.astype(BF16)

    g_wait(0, 1)
    g_start(0, 5)
    g_start(1, 0)
    g_start(1, 1)
    qkv_pair(chip_at(x - 1, y), chip_at(x + 1, y), EARLY)
    g_wait(0, 2)
    g_start(0, 6)
    qkv_pair(chip_at(x, y - 1), chip_at(x, y + 1), EARLY)
    g_wait(0, 3)
    g_start(0, 7)
    g_wait(0, 4)
    g_start(0, 8)

    mine_r = pl.ds(pl.multiple_of(core * CAPC, 16), CAPC)
    theirs_r = pl.ds(pl.multiple_of((1 - core) * CAPC, 16), CAPC)

    def pick(block_of):
        total = jnp.zeros((CAP, LANES), F32)
        for q in range(4):
            total = total + dot_nt(oh[:, q * QUART : (q + 1) * QUART], block_of(q))
        return total.astype(BF16)

    pk[0] = pick(lambda q: jnp.concatenate([xg[chip, 2 * q], xg[chip, 2 * q + 1]], axis=1))
    swap_r = [
        remote(pk.at[i, theirs_r], px.at[i], sends.at[4], recvs.at[4 + i], partner) for i in range(2)
    ]
    swap_r[0].start()

    g_wait(0, 5)
    g_wait(1, 0)
    g_start(1, 2)
    g_start(1, 3)
    g_start(1, 4)
    group1(EARLY)
    g_wait(0, 6)
    g_start(0, 9)
    g_wait(1, 1)
    g_start(1, 5)
    group0(LATE)
    g_wait(0, 7)
    g_wait(0, 8)
    g_wait(1, 2)
    g_start(1, 6)
    g_wait(1, 3)
    g_start(1, 7)
    g_wait(1, 4)
    g_start(1, 8)
    group2(EARLY)
    g_wait(0, 9)
    group3(EARLY)

    def finish_qkv(u):
        scale = lax.rsqrt(jnp.sum(ssq[u], axis=0, keepdims=True) * (1.0 / FEAT) + EPS)
        query = (acc[u, 0:LANES] * scale).astype(BF16).astype(F32) * (1.0 / HEADW**0.5)
        keys = (acc[u, LANES : 2 * LANES] * scale).T.astype(BF16)
        vals = (acc[u, 2 * LANES :] * scale).astype(BF16)
        for half in range(2):
            b = PAIRS[u][half]
            at = slice(half * QBLK, (half + 1) * QBLK)
            qt[:, b * QBLK : (b + 1) * QBLK] = query[:, at].astype(BF16)
            kvb[1 + b, 0] = keys[at]
            kvb[1 + b, 1] = vals[:, at]

    h_prev = remote(kvb.at[1], kvb.at[NBLK + 1], sends.at[5], recvs.at[6], prev_dev)
    h_next = remote(kvb.at[NBLK], kvb.at[0], sends.at[5], recvs.at[7], next_dev)
    finish_qkv(0)
    finish_qkv(1)
    h_prev.start()
    h_next.start()
    g_wait(1, 5)
    g_wait(1, 6)
    g_start(1, 9)
    finish_qkv(2)
    group1(LATE)

    def attend(i, kind):
        at = pl.ds(pl.multiple_of(i * QBLK, QBLK), QBLK)
        q = qt[:, at]
        zero = jnp.zeros((HEADW, QBLK), BF16)
        q2 = jnp.concatenate(
            [jnp.concatenate([q[:HEADW], zero], axis=0), jnp.concatenate([zero, q[HEADW:]], axis=0)], axis=1
        )
        keys = jnp.concatenate([kvb[i, 0], kvb[i + 1, 0], kvb[i + 2, 0]], axis=0)
        vals = jnp.concatenate([kvb[i, 1], kvb[i + 1, 1], kvb[i + 2, 1]], axis=1)
        b = bias[kind]
        s = dot(keys, q2) + jnp.concatenate([b, b], axis=1)
        e = jnp.exp(s - jnp.max(s, axis=0, keepdims=True))
        total = jnp.sum(e, axis=0, keepdims=True)
        o = dot(vals, e.astype(BF16)) / total
        ctx[:, at] = jnp.concatenate([o[:HEADW, :QBLK], o[HEADW:, QBLK:]], axis=0).astype(BF16)

    attend(1, 1)
    attend(NBLK - 2, 1)
    g_wait(1, 7)
    g_wait(1, 8)
    group2(LATE)
    arrived(recvs.at[6], kvb.at[0])
    arrived(recvs.at[7], kvb.at[0])
    attend(0, 0)
    attend(NBLK - 1, 2)

    def wot_rows(index):
        return wot[pl.ds(pl.multiple_of(index * LANES, LANES), LANES), :]

    def project(e, step):
        for h in range(2):
            q = SETS[e][h]
            rhs = ctx[:, q * QUART : (q + 1) * QUART]
            for pair in ((2, -1), (1, 0)):
                i1 = block(h, pair[0], step)
                i2 = block(h, pair[1], step)
                o = dot(jnp.concatenate([wot_rows(i1), wot_rows(i2)], axis=0), rhs).astype(BF16)
                pb[i1, q] = o[:LANES]
                pb[i2, q] = o[LANES:]

    def feats_of(part):
        return slice(part * HEADW, (part + 1) * HEADW)

    def r1_copy(e, h, j, kind, d):
        s = SIGN[d]
        db, part = ((2, d), (s, d), (s, 1 - d))[kind]
        src = pb.at[block(h, OFF[j], db), SETS[e][h], feats_of(part)]
        sem = rrecv.at[e, j if kind == 0 else 4 + j]
        return remote(src, rx1.at[e, h, j, kind, d], sends.at[6], sem, near(h, 1, s))

    def r2_copy(e, h, kind, d):
        s = SIGN[d]
        da, part = ((2, d), (s, d), (s, 1 - d))[kind]
        src = pb.at[block(h, da, 0), SETS[e][h], feats_of(part)]
        sem = rrecv.at[e, 8 if kind == 0 else 9]
        return remote(src, rx2.at[e, h, kind, d], sends.at[6], sem, near(h, 0, s))

    def r1_start(e, j, kind):
        for h, d in both_hd:
            r1_copy(e, h, j, kind, d).start()

    def r2_start(e, kind):
        for h, d in both_hd:
            r2_copy(e, h, kind, d).start()

    def relay1(e, j):
        arrived(rrecv.at[e, j], xg.at[0, 0:4])
        for h, d in both_hd:
            index = block(h, OFF[j], SIGN[d])
            q, at = SETS[e][h], feats_of(d)
            pb[index, q, at] = (pb[index, q, at].astype(F32) + rx1[e, h, j, 0, d].astype(F32)).astype(BF16)
            r1_copy(e, h, j, 1, d).start()

    def relay2(e):
        arrived(rrecv.at[e, 8], xg.at[0, 0:4])
        for h, d in both_hd:
            index = block(h, SIGN[d], 0)
            q, at = SETS[e][h], feats_of(d)
            pb[index, q, at] = (pb[index, q, at].astype(F32) + rx2[e, h, 0, d].astype(F32)).astype(BF16)
            r2_copy(e, h, 1, d).start()

    def sum1(e, h, j, part):
        got = pb[block(h, OFF[j], 0), SETS[e][h], feats_of(part)].astype(F32)
        return got + rx1[e, h, j, 1, part].astype(F32) + rx1[e, h, j, 2, 1 - part].astype(F32)

    def total1(e, j):
        arrived(rrecv.at[e, 4 + j], xg.at[0])
        for h in range(2):
            for part in range(2):
                pb[block(h, OFF[j], 0), SETS[e][h], feats_of(part)] = sum1(e, h, j, part).astype(BF16)

    def last(e):
        arrived(rrecv.at[e, 7], xg.at[0])
        arrived(rrecv.at[e, 9], xg.at[0])
        for h in range(2):
            q = SETS[e][h]
            for part in range(2):
                at = feats_of(part)
                own = jnp.concatenate([xg[chip, 2 * q, at], xg[chip, 2 * q + 1, at]], axis=1)
                mixed = sum1(e, h, 3, part) + rx2[e, h, 1, part].astype(F32) + rx2[e, h, 2, 1 - part].astype(F32)
                upd[q, at] = (own.astype(F32) + mixed).astype(BF16)

    def s1_copy(n, t, j):
        src = sb.at[n, small_block(t, j)]
        return remote(src, rxa.at[n, t - 1, j], sends.at[7], s1recv.at[n, j], small_near(t, 0))

    def s2_copy(n, t):
        src = sb2.at[n, t]
        return remote(src, rxb.at[n, t - 1], sends.at[7], s2recv.at[n], small_near(0, t))

    def o_copy(t):
        dev = {"tp": small_block(0, t) * 2 + 1 - core}
        return remote(sb2.at[1, t], rxo.at[t], sends.at[11], recvs.at[9], dev)

    STEPS = (2, 1, 3)
    COLS = (2, 1, 3, 0)

    def small_start(n):
        for j in COLS:
            for t in STEPS:
                s1_copy(n, t, j).start()

    def small_mid(n):
        for j in COLS:
            total = sb[n, small_block(0, j)].astype(F32)
            arrived(s1recv.at[n, j], sb.at[n, 0:3])
            for t in STEPS:
                total = total + rxa[n, t - 1, j].astype(F32)
            sb2[n, j] = total.astype(BF16)
            if j > 0:
                s2_copy(n, j).start()
            if n == 1:
                o_copy(j).start()

    def small_end(n):
        total = sb2[n, 0].astype(F32)
        arrived(s2recv.at[n], sb.at[n, 0:3])
        for t in STEPS:
            total = total + rxb[n, t - 1].astype(F32)
        return total

    def a_copy(t, j):
        if t == 0:
            src = gp.at[chip, mine_r]
            return remote(src, src, sends.at[8], arecv.at[3 + j], small_near(0, j))
        src = gp.at[small_block(0, -j), mine_r]
        return remote(src, src, sends.at[8], arecv.at[j], small_near(t, 0))

    def f_copy(t, j):
        src = gp.at[small_block(-t, -j), mine_r]
        return remote(src, src, sends.at[9], recvs.at[8], partner)

    def gather_first():
        for j in STEPS:
            a_copy(0, j).start()
        for t in STEPS:
            a_copy(t, 0).start()
        f_copy(0, 0).start()

    def gather_second():
        for j in (1, 3, 2):
            arrived(arecv.at[3 + j], sb.at[0, 0])
            for t in STEPS:
                a_copy(t, j).start()
            f_copy(0, j).start()

    def gather_third():
        for j in (0, 1, 3, 2):
            arrived(arecv.at[j], sb.at[0, 0:3])
            for t in (1, 3, 2):
                f_copy(t, j).start()

    def gather_last():
        arrived(recvs.at[8], sb.at[0])

    project(0, 2)
    r1_start(0, 0, 0)
    r1_start(0, 1, 0)
    r1_start(0, 2, 0)
    project(0, 1)
    project(0, -1)
    r1_start(0, 0, 2)
    g_wait(1, 9)
    group3(LATE)
    finish_qkv(3)
    r1_start(0, 1, 2)
    attend(2, 1)
    attend(3, 1)
    attend(4, 1)
    attend(5, 1)
    pk[1] = pick(lambda q: ctx[:, q * QUART : (q + 1) * QUART])
    swap_r[1].start()
    relay1(0, 0)
    project(1, 2)
    r1_start(0, 2, 2)
    arrived(recvs.at[4], px.at[0])
    arrived(recvs.at[5], px.at[0])
    rows_ctx = (pk[1, mine_r].astype(F32) + px[1].astype(F32)).astype(BF16)
    for k in range(CHIPS // 2):
        o = dot(rows_ctx, wo[:, k * 256 : (k + 1) * 256]).astype(BF16)
        sb[0, 2 * k] = o[:, :LANES]
        sb[0, 2 * k + 1] = o[:, LANES:]
    small_start(0)
    r1_start(0, 3, 0)
    project(0, 0)
    relay1(0, 1)
    relay1(0, 2)
    project(1, 1)
    small_mid(0)
    total1(0, 0)
    r2_start(0, 0)
    r1_start(0, 3, 2)
    r1_start(1, 0, 0)
    project(1, -1)
    rows_new = pk[0, mine_r].astype(F32) + px[0].astype(F32) + small_end(0)
    gp[chip, mine_r] = rows_new.astype(BF16)
    gather_first()
    relay1(0, 3)
    total1(0, 1)
    total1(0, 2)
    r2_start(0, 2)
    r1_start(1, 0, 2)
    r1_start(1, 1, 0)
    project(1, 0)
    gather_second()
    relay1(1, 0)
    r1_start(1, 1, 2)
    r1_start(1, 2, 0)
    r1_start(1, 2, 2)
    gather_third()
    relay2(0)
    r1_start(1, 3, 0)
    relay1(1, 1)
    relay1(1, 2)
    total1(1, 0)
    r2_start(1, 0)
    gather_last()

    sq = jnp.zeros((CAP, LANES), F32)
    for k in range(CHIPS):
        v = gp[k].astype(F32)
        sq = sq + v * v
    scale = lax.rsqrt(jnp.sum(sq, axis=1, keepdims=True) * (1.0 / FEAT) + EPS)
    for k in range(CHIPS):
        at = slice(k * LANES, (k + 1) * LANES)
        nrm[:, at] = (gp[k].astype(F32) * scale * gain_f[at].astype(F32).reshape(1, LANES)).astype(BF16)

    r1_start(1, 3, 2)
    load_fi.wait()

    def ffn_in(n0, nw):
        rows_n = nrm[...]
        gate = dot(rows_n, fi[0, :, n0 : n0 + nw])
        up = dot(rows_n, fi[1, :, n0 : n0 + nw])
        hid[:, n0 : n0 + nw] = (gelu(gate) * up).astype(BF16)

    ffn_in(0, 256)
    total1(1, 1)
    total1(1, 2)
    r2_start(1, 2)
    ffn_in(256, 256)
    relay1(1, 3)
    ffn_in(512, 128)
    relay2(1)
    last(0)
    load_fo.wait()

    def c_copy(n):
        pair = pl.ds(2 * n, 2)
        return remote(pb2.at[pair, theirs_r], rxc.at[pair], sends.at[10], crecv.at[n // 2], partner)

    for n in range(CHIPS // 2):
        o = dot(hid[...], fo[:, n * 256 : (n + 1) * 256]).astype(BF16)
        pb2[2 * n] = o[:, :LANES]
        pb2[2 * n + 1] = o[:, LANES:]
        c_copy(n).start()
    for n in range(4):
        arrived(crecv.at[n], sb.at[0, 0:4])
        for k in range(4 * n, 4 * n + 4):
            sb[1, k] = (pb2[k, mine_r].astype(F32) + rxc[k].astype(F32)).astype(BF16)
    small_start(1)
    last(1)
    small_mid(1)
    heavy = small_end(1)
    arrived(recvs.at[9], sb.at[0, 0:4])
    heavy_oth = rxo[0].astype(F32)
    for t in STEPS:
        heavy_oth = heavy_oth + rxo[t].astype(F32)
    for rows, base_slot, value in ((mine_r, core * CAPC, heavy), (theirs_r, (1 - core) * CAPC, heavy_oth)):
        slot = lax.broadcasted_iota(jnp.int32, (CAPC, LANES), 0) + base_slot
        value = jnp.where(slot < counts[z], value, 0.0)
        high = value.astype(BF16)
        hv[rows, 0:LANES] = high
        hv[rows, LANES:] = (value - high.astype(F32)).astype(BF16)

    for q in range(4):
        at = slice(q * QUART, (q + 1) * QUART)
        added = dot_tn(hv[...], oh[:, at])
        fin[:, at] = (upd[q].astype(F32) + added[:LANES] + added[LANES:]).astype(BF16)
    out_part = out.at[:, pl.ds(pl.multiple_of(core * HALF, HALF), HALF)]
    send_out = remote(fin.at[oth_feat], out_part, sends.at[12], recvs.at[10], partner)
    send_out.start()
    save_out = pltpu.make_async_copy(fin.at[own_feat], out_part, loads.at[5])
    save_out.start()

    left(0, xg.at[0, 0:4])
    left(1, wraw.at[0 : 3 * HEADW])
    left(2, wo.at[0:HEADW])
    left(3, xg.at[0:15])
    left(4, px)
    left(5, kvb.at[0:2])
    left(6, pb.at[0:15])
    left(7, sb.at[:, 0:15])
    left(8, sb.at[0, 0:15])
    left(9, sb.at[0])
    left(10, sb.at[1])
    left(11, sb.at[0, 0:4])
    save_out.wait()
    send_out.wait()


def local(
    residual, attn_gain, attn_in, attn_out, ffn_gain, ffn_in, ffn_out, route_rows, route_counts
):
    any_spec = pl.BlockSpec(memory_space=pl.ANY)
    vm = pltpu.VMEM
    dma = pltpu.SemaphoreType.DMA
    turned = pl.pallas_call(
        kernel,
        out_shape=jax.ShapeDtypeStruct((HEADW, TOK), BF16),
        in_specs=[any_spec] * 5
        + [pl.BlockSpec(memory_space=pltpu.VMEM)] * 3
        + [pl.BlockSpec(memory_space=pltpu.SMEM)],
        out_specs=any_spec,
        scratch_shapes=[
            vm((3 * LANES, FEAT), BF16),
            vm((LANES, FEAT), BF16),
            vm((FEAT, LANES), BF16),
            vm((2, FEAT, FFU), BF16),
            vm((FFU, FEAT), BF16),
            vm((CHIPS, 3 * LANES, LANES), BF16),
            vm((CHIPS, NBLK, LANES, QBLK), BF16),
            vm((4, 3 * LANES, QUART), F32),
            vm((4, 8, QUART), F32),
            vm((LANES, HALF), BF16),
            vm((NBLK + 2, 2, QBLK, QBLK), BF16),
            vm((LANES, HALF), BF16),
            vm((3, 3 * QBLK, QBLK), F32),
            vm((CAP, HALF), BF16),
            vm((CHIPS, 4, LANES, QUART), BF16),
            vm((2, 2, 4, 3, 2, HEADW, QUART), BF16),
            vm((2, 2, 3, 2, HEADW, QUART), BF16),
            vm((4, LANES, QUART), BF16),
            vm((LANES, HALF), BF16),
            vm((CHIPS, CAP, LANES), BF16),
            vm((2, CAP, LANES), BF16),
            vm((2, CAPC, LANES), BF16),
            vm((CAP, FEAT), BF16),
            vm((CAP, FFU), BF16),
            vm((CHIPS, CAP, LANES), BF16),
            vm((CHIPS, CAPC, LANES), BF16),
            vm((2, CHIPS, CAPC, LANES), BF16),
            vm((2, 3, SIDE, CAPC, LANES), BF16),
            vm((2, SIDE, CAPC, LANES), BF16),
            vm((2, 3, CAPC, LANES), BF16),
            vm((SIDE, CAPC, LANES), BF16),
            vm((CAP, 2 * LANES), BF16),
            dma((6,)),
            dma((13,)),
            dma((11,)),
            dma((2, 10)),
            dma((2, 10)),
            dma((2, SIDE)),
            dma((2,)),
            dma((7,)),
            dma((4,)),
        ],
        compiler_params=pltpu.CompilerParams(
            collective_id=0, has_side_effects=True, vmem_limit_bytes=62 * 1024 * 1024
        ),
        name="layer",
    )(
        residual.T, attn_in.transpose(0, 2, 1), attn_out, ffn_in, ffn_out, attn_gain, ffn_gain, route_rows, route_counts
    )
    return turned.T


def solution(mesh):
    in_specs = (
        P("seq", "tp"),
        P(),
        P(None, None, "tp"),
        P("tp", None),
        P(),
        P(None, None, "tp"),
        P("tp", None),
        P("seq", None),
        P(),
    )
    out_specs = P("seq", "tp")
    return jax.shard_map(local, mesh=mesh, in_specs=in_specs, out_specs=out_specs, check_vma=False)
```

```python
import jax
import jax.numpy as jnp
from jax import lax
from jax.experimental import pallas as pl
from jax.experimental.pallas import tpu as pltpu
from jax.sharding import PartitionSpec as P

MESH = pl.DeviceIdType.MESH
F32 = jnp.float32
BF16 = jnp.bfloat16
EPS = 1e-06
RADIUS = 127
NEG = -1e30
SIDE = 4
CHIPS = SIDE * SIDE
TOK = 2048
HALF = TOK // 2
QUART = HALF // 4
LANES = 128
FEAT = CHIPS * LANES
HEADW = 64
CAP = 224
CAPC = CAP // 2
FFU = 640
QBLK = 128
NBLK = HALF // QBLK
OFF = (2, -1, 1, 0)
SIGN = (1, -1)
CHUNK = (((0, 3), (5, 3)), ((3, 1), (4, 1)))
PAIRS = ((0, 1), (6, 7), (2, 5), (3, 4))
SETS = ((0, 3), (1, 2))


def gelu(v):
    return 0.5 * v * (1.0 + jnp.tanh(0.7978845608028654 * (v + 0.044715 * v * v * v)))


def dot(a, b):
    return jnp.dot(a, b, preferred_element_type=F32)


def dot_nt(a, b):
    return lax.dot_general(a, b, (((1,), (1,)), ((), ())), preferred_element_type=F32)


def dot_tn(a, b):
    return lax.dot_general(a, b, (((0,), (0,)), ((), ())), preferred_element_type=F32)


def kernel(
    res, wqkv, wout, ffi, ffo, gain_a_in, gain_f_in, route_in, counts,
    out,
    gain_a, gain_f, route, updx, wraw, wo, wot, fi, fo, w2, xg, acc, ssq, qt, kvb, ctx, bias, oh,
    pb, rx1, rx2, upd, fin, gp, pk, px, nrm, hid, pb2, rxc, sb, rxa, sb2, rxb, rxo, hv,
    loads, sends, recvs, grecv, rrecv, s1recv, s2recv, arecv, crecv,
):
    z = lax.axis_index("seq")
    tp = lax.axis_index("tp")
    core = lax.rem(tp, 2)
    chip = tp // 2
    x = lax.rem(chip, SIDE)
    y = chip // SIDE
    partner = {"tp": tp + 1 - 2 * core}

    def wrap(v):
        return lax.rem(v + 2 * SIDE, SIDE)

    def chip_at(cx, cy):
        return wrap(cy) * SIDE + wrap(cx)

    def tp_at(cx, cy):
        return chip_at(cx, cy) * 2 + core

    def remote(src, dst, ssem, rsem, dev):
        return pltpu.make_async_remote_copy(
            src_ref=src, dst_ref=dst, send_sem=ssem, recv_sem=rsem, device_id=dev, device_id_type=MESH
        )

    def arrived(sem, ref):
        remote(ref, ref, sends.at[0], sem, partner).wait_recv()

    def left(n, ref):
        remote(ref, ref, sends.at[n], recvs.at[0], partner).wait_send()

    def block(h, da, db):
        return chip_at(x + da, y + db) if h == 0 else chip_at(x + db, y + da)

    def near(h, axis, step):
        if (axis == 0) == (h == 0):
            return {"tp": tp_at(x + step, y)}
        return {"tp": tp_at(x, y + step)}

    def small_block(da, db):
        return chip_at(x + da + core * (db - da), y + db + core * (da - db))

    def small_near(da, db):
        return {"tp": small_block(da, db) * 2 + core}

    first = core == 0
    own_feat = pl.ds(pl.multiple_of(core * HEADW, HEADW), HEADW)
    oth_feat = pl.ds(pl.multiple_of((1 - core) * HEADW, HEADW), HEADW)

    def tokens(half, b):
        return pl.ds(pl.multiple_of(half * HALF + b * QBLK, QBLK), QBLK)

    ORDER = (0, 1, 2, 5, 6, 7, 3, 4)

    def w_rows(p):
        return pl.ds(pl.multiple_of(p * LANES + core * HEADW, HEADW), HEADW)

    load_x = [
        pltpu.make_async_copy(res.at[:, tokens(core, b)], xg.at[chip, b, own_feat], loads.at[0]) for b in ORDER
    ]
    load_w = [pltpu.make_async_copy(wqkv.at[p], wraw.at[w_rows(p)], loads.at[1]) for p in range(3)]
    load_o = pltpu.make_async_copy(wout, wo.at[own_feat], loads.at[2])
    load_fi = pltpu.make_async_copy(ffi, fi, loads.at[3])
    load_fo = pltpu.make_async_copy(ffo, fo, loads.at[4])
    for copy in load_x + load_w:
        copy.start()
    load_o.start()
    load_small = [
        pltpu.make_async_copy(src, dst, loads.at[6 + i])
        for i, (src, dst) in enumerate(((gain_a_in, gain_a), (gain_f_in, gain_f), (route_in, route)))
    ]
    for copy in load_small:
        copy.start()

    other = tp + 1 - 2 * core
    prev_dev = {"seq": lax.rem(z + 3 + core, 4), "tp": other}
    next_dev = {"seq": lax.rem(z + core, 4), "tp": other}
    z_peer = {"seq": lax.rem(z + 3 + 2 * core, 4), "tp": other}
    barrier = pltpu.get_barrier_semaphore()
    peers = [near(0, 0, 1), near(0, 0, -1), near(0, 1, 1), near(0, 1, -1), partner, z_peer]
    for dev in peers:
        pl.semaphore_signal(barrier, inc=1, device_id=dev, device_id_type=MESH)
    pl.semaphore_wait(barrier, len(peers))

    swap_x = [
        remote(
            res.at[:, tokens(1 - core, b)], xg.at[chip, b, own_feat], sends.at[0],
            recvs.at[1 if b in (3, 4) else 0], partner,
        )
        for b in ORDER
    ]
    swap_w = [
        remote(wqkv.at[p], wraw.at[w_rows(p)], sends.at[1], recvs.at[2], partner) for p in range(3)
    ]
    swap_o = remote(wout, wo.at[own_feat], sends.at[2], recvs.at[3], partner)
    for copy in swap_x + swap_w:
        copy.start()
    swap_o.start()

    def g_item(c, h, item, d, piece=None):
        s = SIGN[d]
        index, part, axis = {
            0: (block(h, 0, 0), None, 0),
            1: (block(h, 0, 0), None, 1),
            2: (block(h, -s, 0), d, 0),
            3: (block(h, -1, 0), None, 1),
            4: (block(h, 1, 0), None, 1),
            5: (block(h, 0, -s), d, 1),
            6: (block(h, 2, 0), None, 1),
            7: (block(h, -1, -s), d, 1),
            8: (block(h, 1, -s), d, 1),
            9: (block(h, 2, -s), d, 1),
        }[item]
        feats = pl.ds(0, LANES) if part is None else pl.ds(part * HEADW, HEADW)
        if piece is not None:
            feats = (own_feat, oth_feat)[piece]
        start, count = CHUNK[c][h]
        src = xg.at[index, pl.ds(start, count), feats]
        return remote(src, src, sends.at[3], grecv.at[c, item], near(h, axis, s))

    both_hd = [(h, d) for h in range(2) for d in range(2)]

    def g_start(c, item, piece=None):
        for h, d in both_hd:
            g_item(c, h, item, d, piece).start()

    def g_wait(c, item):
        count = CHUNK[c][0][1] * 2
        if item in (0, 1, 3, 4, 6):
            arrived(grecv.at[c, item], xg.at[0:2, 0:count])
        else:
            arrived(grecv.at[c, item], xg.at[0, 0:count])

    pltpu.make_async_copy(xg.at[0, 0:4], xg.at[0, 0:4], loads.at[0]).wait()
    g_start(0, 0, 0)
    g_start(0, 1, 0)
    arrived(recvs.at[0], xg.at[0, 0:3])
    g_start(0, 0, 1)
    g_start(0, 1, 1)
    arrived(recvs.at[1], xg.at[0, 0])
    load_fi.start()
    load_fo.start()

    for copy in load_small:
        copy.wait()

    pltpu.make_async_copy(wraw.at[0 : 3 * HEADW], wraw.at[0 : 3 * HEADW], loads.at[1]).wait()
    arrived(recvs.at[2], wraw.at[0 : 3 * HEADW])
    for k in range(CHIPS):
        cols = slice(k * LANES, (k + 1) * LANES)
        w2[k] = (wraw[:, cols].astype(F32) * gain_a[cols].astype(F32).reshape(1, LANES)).astype(BF16)

    g_wait(0, 0)
    g_start(0, 2)
    g_start(0, 3)
    g_start(0, 4)

    acc[...] = jnp.zeros_like(acc)
    ssq[...] = jnp.zeros_like(ssq)

    def qkv_pair(i1, i2, pairs):
        wpair = jnp.concatenate([w2[i1], w2[i2]], axis=1)
        for u in pairs:
            b1, b2 = PAIRS[u]
            x1 = jnp.concatenate([xg[i1, b1], xg[i1, b2]], axis=1)
            x2 = jnp.concatenate([xg[i2, b1], xg[i2, b2]], axis=1)
            xx = jnp.concatenate([x1, x2], axis=0)
            acc[u] += dot(wpair, xx)
            f = xx.astype(F32)
            ssq[u] += jnp.sum((f * f).reshape(2 * LANES // 8, 8, QUART), axis=0)

    def group0(pairs):
        qkv_pair(chip_at(x - 1, y), chip_at(x + 1, y), pairs)
        qkv_pair(chip_at(x, y - 1), chip_at(x, y + 1), pairs)

    def group1(pairs):
        qkv_pair(chip_at(x - 1, y - 1), chip_at(x + 1, y - 1), pairs)
        qkv_pair(chip_at(x - 1, y + 1), chip_at(x + 1, y + 1), pairs)
        qkv_pair(chip_at(x + 2, y), chip_at(x, y + 2), pairs)

    def group2(pairs):
        qkv_pair(chip_at(x + 2, y - 1), chip_at(x + 2, y + 1), pairs)
        qkv_pair(chip_at(x - 1, y + 2), chip_at(x + 1, y + 2), pairs)

    def group3(pairs):
        qkv_pair(chip, chip_at(x + 2, y + 2), pairs)

    EARLY = (0, 1, 2)
    LATE = (3,)

    row = route[...].astype(F32)
    r_i = lax.broadcasted_iota(jnp.int32, (CAP, CAP), 0)
    c_i = lax.broadcasted_iota(jnp.int32, (CAP, CAP), 1)
    col = jnp.sum(jnp.where(r_i == c_i, row, 0.0), axis=1, keepdims=True)
    lane = lax.broadcasted_iota(jnp.int32, (CAP, TOK), 1).astype(F32)
    oh[...] = jnp.where(lane == col, 1.0, 0.0).astype(BF16)
    k_i = lax.broadcasted_iota(jnp.int32, (3 * QBLK, QBLK), 0) - QBLK
    q_i = lax.broadcasted_iota(jnp.int32, (3 * QBLK, QBLK), 1)
    band = jnp.where(jnp.abs(q_i - k_i) <= RADIUS, 0.0, NEG)
    bias[0] = band + jnp.where(k_i < 0, jnp.where(z + core == 0, NEG, 0.0), 0.0)
    bias[1] = band
    bias[2] = band + jnp.where(k_i >= QBLK, jnp.where(z + core == 4, NEG, 0.0), 0.0)
    load_o.wait()
    arrived(recvs.at[3], wo.at[0:HEADW])
    for k in range(CHIPS):
        at = slice(k * LANES, (k + 1) * LANES)
        wot[at] = wo[:, at].astype(F32).T.astype(BF16)

    g_wait(0, 1)
    g_start(0, 5)
    g_start(1, 0)
    g_start(1, 1)
    qkv_pair(chip_at(x - 1, y), chip_at(x + 1, y), EARLY)
    g_wait(0, 2)
    g_start(0, 6)
    qkv_pair(chip_at(x, y - 1), chip_at(x, y + 1), EARLY)
    g_wait(0, 3)
    g_start(0, 7)
    g_wait(0, 4)
    g_start(0, 8)

    mine_r = pl.ds(pl.multiple_of(core * CAPC, 16), CAPC)
    theirs_r = pl.ds(pl.multiple_of((1 - core) * CAPC, 16), CAPC)

    def quart_of(half, q):
        return pl.ds(pl.multiple_of(half * HALF + q * QUART, QUART), QUART)

    def pick(block_of):
        total = jnp.zeros((CAP, LANES), F32)
        for q in range(4):
            total = total + dot_nt(oh[:, quart_of(core, q)], block_of(q))
        return total.astype(BF16)

    pk[0] = pick(lambda q: jnp.concatenate([xg[chip, 2 * q], xg[chip, 2 * q + 1]], axis=1))
    swap_r = [
        remote(pk.at[i, theirs_r], px.at[i], sends.at[4], recvs.at[4 + i], partner) for i in range(2)
    ]
    swap_r[0].start()

    g_wait(0, 5)
    g_wait(1, 0)
    g_start(1, 2)
    g_start(1, 3)
    g_start(1, 4)
    group1(EARLY)
    g_wait(0, 6)
    g_start(0, 9)
    g_wait(1, 1)
    g_start(1, 5)
    group0(LATE)
    g_wait(0, 7)
    g_wait(0, 8)
    g_wait(1, 2)
    g_start(1, 6)
    g_wait(1, 3)
    g_start(1, 7)
    g_wait(1, 4)
    g_start(1, 8)
    group2(EARLY)
    g_wait(0, 9)
    group3(EARLY)

    def finish_qkv(u):
        scale = lax.rsqrt(jnp.sum(ssq[u], axis=0, keepdims=True) * (1.0 / FEAT) + EPS)
        query = (acc[u, 0:LANES] * scale).astype(BF16).astype(F32) * (1.0 / HEADW**0.5)
        keys = (acc[u, LANES : 2 * LANES] * scale).T.astype(BF16)
        vals = (acc[u, 2 * LANES :] * scale).astype(BF16)
        for half in range(2):
            b = PAIRS[u][half]
            at = slice(half * QBLK, (half + 1) * QBLK)
            qt[:, b * QBLK : (b + 1) * QBLK] = query[:, at].astype(BF16)
            kvb[1 + b, 0] = keys[at]
            kvb[1 + b, 1] = vals[:, at]

    h_prev = remote(kvb.at[1], kvb.at[NBLK + 1], sends.at[5], recvs.at[6], prev_dev)
    h_next = remote(kvb.at[NBLK], kvb.at[0], sends.at[5], recvs.at[7], next_dev)
    finish_qkv(0)
    finish_qkv(1)
    h_prev.start()
    h_next.start()
    g_wait(1, 5)
    g_wait(1, 6)
    g_start(1, 9)
    finish_qkv(2)
    group1(LATE)

    def attend(i, kind):
        at = pl.ds(pl.multiple_of(i * QBLK, QBLK), QBLK)
        q = qt[:, at]
        zero = jnp.zeros((HEADW, QBLK), BF16)
        q2 = jnp.concatenate(
            [jnp.concatenate([q[:HEADW], zero], axis=0), jnp.concatenate([zero, q[HEADW:]], axis=0)], axis=1
        )
        keys = jnp.concatenate([kvb[i, 0], kvb[i + 1, 0], kvb[i + 2, 0]], axis=0)
        vals = jnp.concatenate([kvb[i, 1], kvb[i + 1, 1], kvb[i + 2, 1]], axis=1)
        b = bias[kind]
        s = dot(keys, q2) + jnp.concatenate([b, b], axis=1)
        e = jnp.exp(s - jnp.max(s, axis=0, keepdims=True))
        total = jnp.sum(e, axis=0, keepdims=True)
        o = dot(vals, e.astype(BF16)) / total
        ctx[:, at] = jnp.concatenate([o[:HEADW, :QBLK], o[HEADW:, QBLK:]], axis=0).astype(BF16)

    attend(1, 1)
    attend(NBLK - 2, 1)
    g_wait(1, 7)
    g_wait(1, 8)
    group2(LATE)
    arrived(recvs.at[6], kvb.at[0])
    arrived(recvs.at[7], kvb.at[0])
    attend(0, 0)
    attend(NBLK - 1, 2)

    def wot_rows(index):
        return wot[pl.ds(pl.multiple_of(index * LANES, LANES), LANES), :]

    def project(e, step):
        for h in range(2):
            q = SETS[e][h]
            rhs = ctx[:, q * QUART : (q + 1) * QUART]
            for pair in ((2, -1), (1, 0)):
                i1 = block(h, pair[0], step)
                i2 = block(h, pair[1], step)
                o = dot(jnp.concatenate([wot_rows(i1), wot_rows(i2)], axis=0), rhs).astype(BF16)
                pb[i1, q] = o[:LANES]
                pb[i2, q] = o[LANES:]

    def feats_of(part):
        return slice(part * HEADW, (part + 1) * HEADW)

    def r1_copy(e, h, j, kind, d):
        s = SIGN[d]
        db, part = ((2, d), (s, d), (s, 1 - d))[kind]
        src = pb.at[block(h, OFF[j], db), SETS[e][h], feats_of(part)]
        sem = rrecv.at[e, j if kind == 0 else 4 + j]
        return remote(src, rx1.at[e, h, j, kind, d], sends.at[6], sem, near(h, 1, s))

    def r2_copy(e, h, kind, d):
        s = SIGN[d]
        da, part = ((2, d), (s, d), (s, 1 - d))[kind]
        src = pb.at[block(h, da, 0), SETS[e][h], feats_of(part)]
        sem = rrecv.at[e, 8 if kind == 0 else 9]
        return remote(src, rx2.at[e, h, kind, d], sends.at[6], sem, near(h, 0, s))

    def r1_start(e, j, kind):
        for h, d in both_hd:
            r1_copy(e, h, j, kind, d).start()

    def r2_start(e, kind):
        for h, d in both_hd:
            r2_copy(e, h, kind, d).start()

    def relay1(e, j):
        arrived(rrecv.at[e, j], xg.at[0, 0:4])
        for h, d in both_hd:
            index = block(h, OFF[j], SIGN[d])
            q, at = SETS[e][h], feats_of(d)
            pb[index, q, at] = (pb[index, q, at].astype(F32) + rx1[e, h, j, 0, d].astype(F32)).astype(BF16)
            r1_copy(e, h, j, 1, d).start()

    def relay2(e):
        arrived(rrecv.at[e, 8], xg.at[0, 0:4])
        for h, d in both_hd:
            index = block(h, SIGN[d], 0)
            q, at = SETS[e][h], feats_of(d)
            pb[index, q, at] = (pb[index, q, at].astype(F32) + rx2[e, h, 0, d].astype(F32)).astype(BF16)
            r2_copy(e, h, 1, d).start()

    def sum1(e, h, j, part):
        got = pb[block(h, OFF[j], 0), SETS[e][h], feats_of(part)].astype(F32)
        return got + rx1[e, h, j, 1, part].astype(F32) + rx1[e, h, j, 2, 1 - part].astype(F32)

    def total1(e, j):
        arrived(rrecv.at[e, 4 + j], xg.at[0])
        for h in range(2):
            for part in range(2):
                pb[block(h, OFF[j], 0), SETS[e][h], feats_of(part)] = sum1(e, h, j, part).astype(BF16)

    def last(e):
        arrived(rrecv.at[e, 7], xg.at[0])
        arrived(rrecv.at[e, 9], xg.at[0])
        for h in range(2):
            q = SETS[e][h]
            for part in range(2):
                at = feats_of(part)
                own = jnp.concatenate([xg[chip, 2 * q, at], xg[chip, 2 * q + 1, at]], axis=1)
                mixed = sum1(e, h, 3, part) + rx2[e, h, 1, part].astype(F32) + rx2[e, h, 2, 1 - part].astype(F32)
                upd[q, at] = (own.astype(F32) + mixed).astype(BF16)

    def s1_copy(n, t, j):
        src = sb.at[n, small_block(t, j)]
        return remote(src, rxa.at[n, t - 1, j], sends.at[7], s1recv.at[n, j], small_near(t, 0))

    def s2_copy(n, t):
        src = sb2.at[n, t]
        return remote(src, rxb.at[n, t - 1], sends.at[7], s2recv.at[n], small_near(0, t))

    def o_copy(t):
        dev = {"tp": small_block(0, t) * 2 + 1 - core}
        return remote(sb2.at[1, t], rxo.at[t], sends.at[11], recvs.at[9], dev)

    STEPS = (2, 1, 3)
    COLS = (2, 1, 3, 0)

    def small_start(n):
        for j in COLS:
            for t in STEPS:
                s1_copy(n, t, j).start()

    def small_mid(n):
        for j in COLS:
            total = sb[n, small_block(0, j)].astype(F32)
            arrived(s1recv.at[n, j], sb.at[n, 0:3])
            for t in STEPS:
                total = total + rxa[n, t - 1, j].astype(F32)
            sb2[n, j] = total.astype(BF16)
            if j > 0:
                s2_copy(n, j).start()
            if n == 1:
                o_copy(j).start()

    def small_end(n):
        total = sb2[n, 0].astype(F32)
        arrived(s2recv.at[n], sb.at[n, 0:3])
        for t in STEPS:
            total = total + rxb[n, t - 1].astype(F32)
        return total

    def a_copy(t, j):
        if t == 0:
            src = gp.at[chip, mine_r]
            return remote(src, src, sends.at[8], arecv.at[3 + j], small_near(0, j))
        src = gp.at[small_block(0, -j), mine_r]
        return remote(src, src, sends.at[8], arecv.at[j], small_near(t, 0))

    def f_copy(t, j):
        src = gp.at[small_block(-t, -j), mine_r]
        return remote(src, src, sends.at[9], recvs.at[8], partner)

    def gather_first():
        for j in STEPS:
            a_copy(0, j).start()
        for t in STEPS:
            a_copy(t, 0).start()
        f_copy(0, 0).start()

    def gather_second():
        for j in (1, 3, 2):
            arrived(arecv.at[3 + j], sb.at[0, 0])
            for t in STEPS:
                a_copy(t, j).start()
            f_copy(0, j).start()

    def gather_third():
        for j in (0, 1, 3, 2):
            arrived(arecv.at[j], sb.at[0, 0:3])
            for t in (1, 3, 2):
                f_copy(t, j).start()

    def gather_last():
        arrived(recvs.at[8], sb.at[0])

    project(0, 2)
    r1_start(0, 0, 0)
    r1_start(0, 1, 0)
    r1_start(0, 2, 0)
    project(0, 1)
    project(0, -1)
    r1_start(0, 0, 2)
    g_wait(1, 9)
    group3(LATE)
    finish_qkv(3)
    r1_start(0, 1, 2)
    attend(2, 1)
    attend(3, 1)
    attend(4, 1)
    attend(5, 1)
    pk[1] = pick(lambda q: ctx[:, q * QUART : (q + 1) * QUART])
    swap_r[1].start()
    relay1(0, 0)
    project(1, 2)
    r1_start(0, 2, 2)
    arrived(recvs.at[4], px.at[0])
    arrived(recvs.at[5], px.at[0])
    rows_ctx = (pk[1, mine_r].astype(F32) + px[1].astype(F32)).astype(BF16)
    for k in range(CHIPS // 2):
        o = dot(rows_ctx, wo[:, k * 256 : (k + 1) * 256]).astype(BF16)
        sb[0, 2 * k] = o[:, :LANES]
        sb[0, 2 * k + 1] = o[:, LANES:]
    small_start(0)
    r1_start(0, 3, 0)
    project(0, 0)
    relay1(0, 1)
    relay1(0, 2)
    project(1, 1)
    small_mid(0)
    total1(0, 0)
    r2_start(0, 0)
    r1_start(0, 3, 2)
    r1_start(1, 0, 0)
    project(1, -1)
    rows_new = pk[0, mine_r].astype(F32) + px[0].astype(F32) + small_end(0)
    gp[chip, mine_r] = rows_new.astype(BF16)
    gather_first()
    relay1(0, 3)
    total1(0, 1)
    total1(0, 2)
    r2_start(0, 2)
    r1_start(1, 0, 2)
    r1_start(1, 1, 0)
    project(1, 0)
    gather_second()
    relay1(1, 0)
    r1_start(1, 1, 2)
    r1_start(1, 2, 0)
    r1_start(1, 2, 2)
    gather_third()
    relay2(0)
    r1_start(1, 3, 0)
    relay1(1, 1)
    relay1(1, 2)
    total1(1, 0)
    r2_start(1, 0)
    gather_last()

    sq = jnp.zeros((CAP, LANES), F32)
    for k in range(CHIPS):
        v = gp[k].astype(F32)
        sq = sq + v * v
    scale = lax.rsqrt(jnp.sum(sq, axis=1, keepdims=True) * (1.0 / FEAT) + EPS)
    for k in range(CHIPS):
        at = slice(k * LANES, (k + 1) * LANES)
        nrm[:, at] = (gp[k].astype(F32) * scale * gain_f[at].astype(F32).reshape(1, LANES)).astype(BF16)

    r1_start(1, 3, 2)
    load_fi.wait()

    def ffn_in(n0, nw):
        rows_n = nrm[...]
        gate = dot(rows_n, fi[0, :, n0 : n0 + nw])
        up = dot(rows_n, fi[1, :, n0 : n0 + nw])
        hid[:, n0 : n0 + nw] = (gelu(gate) * up).astype(BF16)

    ffn_in(0, 256)
    total1(1, 1)
    total1(1, 2)
    r2_start(1, 2)
    ffn_in(256, 256)
    relay1(1, 3)
    ffn_in(512, 128)
    relay2(1)
    last(0)
    load_fo.wait()

    def c_copy(n):
        pair = pl.ds(2 * n, 2)
        return remote(pb2.at[pair, theirs_r], rxc.at[pair], sends.at[10], crecv.at[n // 2], partner)

    for n in range(CHIPS // 2):
        o = dot(hid[...], fo[:, n * 256 : (n + 1) * 256]).astype(BF16)
        pb2[2 * n] = o[:, :LANES]
        pb2[2 * n + 1] = o[:, LANES:]
        c_copy(n).start()
    for n in range(4):
        arrived(crecv.at[n], sb.at[0, 0:4])
        for k in range(4 * n, 4 * n + 4):
            sb[1, k] = (pb2[k, mine_r].astype(F32) + rxc[k].astype(F32)).astype(BF16)
    small_start(1)
    last(1)
    swap_u = remote(upd.at[:, oth_feat], updx, sends.at[12], recvs.at[10], partner)
    swap_u.start()
    small_mid(1)
    heavy = small_end(1)
    arrived(recvs.at[9], sb.at[0, 0:4])
    heavy_oth = rxo[0].astype(F32)
    for t in STEPS:
        heavy_oth = heavy_oth + rxo[t].astype(F32)
    for rows, base_slot, value in ((mine_r, core * CAPC, heavy), (theirs_r, (1 - core) * CAPC, heavy_oth)):
        slot = lax.broadcasted_iota(jnp.int32, (CAPC, LANES), 0) + base_slot
        value = jnp.where(slot < counts[z], value, 0.0)
        high = value.astype(BF16)
        low = (value - high.astype(F32)).astype(BF16)
        hv[rows, :] = jnp.concatenate(
            [
                jnp.where(first, high[:, :HEADW], high[:, HEADW:]),
                jnp.where(first, low[:, :HEADW], low[:, HEADW:]),
            ],
            axis=1,
        )

    arrived(recvs.at[10], updx)
    for q in range(4):
        for half, rows_now in ((core, upd[q, own_feat]), (1 - core, updx[q])):
            at = quart_of(half, q)
            added = dot_tn(hv[...], oh[:, at])
            fin[:, at] = (rows_now.astype(F32) + added[:HEADW] + added[HEADW:]).astype(BF16)
    save_out = pltpu.make_async_copy(fin, out, loads.at[5])
    save_out.start()

    left(0, xg.at[0, 0:4])
    left(1, wraw.at[0 : 3 * HEADW])
    left(2, wo.at[0:HEADW])
    left(3, xg.at[0:15])
    left(4, px)
    left(5, kvb.at[0:2])
    left(6, pb.at[0:15])
    left(7, sb.at[:, 0:15])
    left(8, sb.at[0, 0:15])
    left(9, sb.at[0])
    left(10, sb.at[1])
    left(11, sb.at[0, 0:4])
    left(12, updx)
    save_out.wait()


def local(
    residual, attn_gain, attn_in, attn_out, ffn_gain, ffn_in, ffn_out, route_rows, route_counts
):
    any_spec = pl.BlockSpec(memory_space=pl.ANY)
    vm = pltpu.VMEM
    dma = pltpu.SemaphoreType.DMA
    turned = pl.pallas_call(
        kernel,
        out_shape=jax.ShapeDtypeStruct((HEADW, TOK), BF16),
        in_specs=[any_spec] * 8
        + [pl.BlockSpec(memory_space=pltpu.SMEM)],
        out_specs=any_spec,
        scratch_shapes=[
            vm((FEAT,), BF16),
            vm((FEAT,), BF16),
            vm((1, CAP), jnp.int32),
            vm((4, HEADW, QUART), BF16),
            vm((3 * LANES, FEAT), BF16),
            vm((LANES, FEAT), BF16),
            vm((FEAT, LANES), BF16),
            vm((2, FEAT, FFU), BF16),
            vm((FFU, FEAT), BF16),
            vm((CHIPS, 3 * LANES, LANES), BF16),
            vm((CHIPS, NBLK, LANES, QBLK), BF16),
            vm((4, 3 * LANES, QUART), F32),
            vm((4, 8, QUART), F32),
            vm((LANES, HALF), BF16),
            vm((NBLK + 2, 2, QBLK, QBLK), BF16),
            vm((LANES, HALF), BF16),
            vm((3, 3 * QBLK, QBLK), F32),
            vm((CAP, TOK), BF16),
            vm((CHIPS, 4, LANES, QUART), BF16),
            vm((2, 2, 4, 3, 2, HEADW, QUART), BF16),
            vm((2, 2, 3, 2, HEADW, QUART), BF16),
            vm((4, LANES, QUART), BF16),
            vm((HEADW, TOK), BF16),
            vm((CHIPS, CAP, LANES), BF16),
            vm((2, CAP, LANES), BF16),
            vm((2, CAPC, LANES), BF16),
            vm((CAP, FEAT), BF16),
            vm((CAP, FFU), BF16),
            vm((CHIPS, CAP, LANES), BF16),
            vm((CHIPS, CAPC, LANES), BF16),
            vm((2, CHIPS, CAPC, LANES), BF16),
            vm((2, 3, SIDE, CAPC, LANES), BF16),
            vm((2, SIDE, CAPC, LANES), BF16),
            vm((2, 3, CAPC, LANES), BF16),
            vm((SIDE, CAPC, LANES), BF16),
            vm((CAP, LANES), BF16),
            dma((9,)),
            dma((13,)),
            dma((11,)),
            dma((2, 10)),
            dma((2, 10)),
            dma((2, SIDE)),
            dma((2,)),
            dma((7,)),
            dma((4,)),
        ],
        compiler_params=pltpu.CompilerParams(
            collective_id=0, has_side_effects=True, vmem_limit_bytes=62 * 1024 * 1024
        ),
        name="layer",
    )(
        residual.T, attn_in.transpose(0, 2, 1), attn_out, ffn_in, ffn_out, attn_gain, ffn_gain, route_rows, route_counts
    )
    return turned.T


def solution(mesh):
    in_specs = (
        P("seq", "tp"),
        P(),
        P(None, None, "tp"),
        P("tp", None),
        P(),
        P(None, None, "tp"),
        P("tp", None),
        P("seq", None),
        P(),
    )
    out_specs = P("seq", "tp")
    return jax.shard_map(local, mesh=mesh, in_specs=in_specs, out_specs=out_specs, check_vma=False)
```

```python
import jax
import jax.numpy as jnp
from jax import lax
from jax.experimental import pallas as pl
from jax.experimental.pallas import tpu as pltpu
from jax.sharding import PartitionSpec as P

MESH = pl.DeviceIdType.MESH
F32 = jnp.float32
BF16 = jnp.bfloat16
EPS = 1e-06
RADIUS = 127
NEG = -1e30
SIDE = 4
CHIPS = SIDE * SIDE
TOK = 2048
HALF = TOK // 2
QUART = HALF // 4
LANES = 128
FEAT = CHIPS * LANES
HEADW = 64
CAP = 224
CAPC = CAP // 2
FFU = 640
QBLK = 128
NBLK = HALF // QBLK
OFF = (2, -1, 1, 0)
SIGN = (1, -1)
CHUNK = (((0, 3), (5, 3)), ((3, 1), (4, 1)))
PAIRS = ((0, 1), (6, 7), (2, 5), (3, 4))
SETS = ((0, 3), (1, 2))


def gelu(v):
    return 0.5 * v * (1.0 + jnp.tanh(0.7978845608028654 * (v + 0.044715 * v * v * v)))


def dot(a, b):
    return jnp.dot(a, b, preferred_element_type=F32)


def dot_nt(a, b):
    return lax.dot_general(a, b, (((1,), (1,)), ((), ())), preferred_element_type=F32)


def dot_tn(a, b):
    return lax.dot_general(a, b, (((0,), (0,)), ((), ())), preferred_element_type=F32)


def kernel(
    res, wqkv, wout, ffi, ffo, gain_a_in, gain_f_in, route_in, counts,
    out,
    gain_a, gain_f, route, updx, wraw, wo, wot, fi, fo, w2, xg, acc, ssq, qt, kvb, ctx, bias, oh,
    pb, rx1, rx2, upd, fin, gp, pk, px, nrm, hid, pb2, rxc, sb, rxa, sb2, rxb, rxo, hv,
    loads, sends, recvs, grecv, rrecv, s1recv, s2recv, arecv, crecv,
):
    z = lax.axis_index("seq")
    tp = lax.axis_index("tp")
    core = lax.rem(tp, 2)
    chip = tp // 2
    x = lax.rem(chip, SIDE)
    y = chip // SIDE
    partner = {"tp": tp + 1 - 2 * core}

    def wrap(v):
        return lax.rem(v + 2 * SIDE, SIDE)

    def chip_at(cx, cy):
        return wrap(cy) * SIDE + wrap(cx)

    def tp_at(cx, cy):
        return chip_at(cx, cy) * 2 + core

    def remote(src, dst, ssem, rsem, dev):
        return pltpu.make_async_remote_copy(
            src_ref=src, dst_ref=dst, send_sem=ssem, recv_sem=rsem, device_id=dev, device_id_type=MESH
        )

    def arrived(sem, ref):
        remote(ref, ref, sends.at[0], sem, partner).wait_recv()

    def left(n, ref):
        remote(ref, ref, sends.at[n], recvs.at[0], partner).wait_send()

    def block(h, da, db):
        return chip_at(x + da, y + db) if h == 0 else chip_at(x + db, y + da)

    def near(h, axis, step):
        if (axis == 0) == (h == 0):
            return {"tp": tp_at(x + step, y)}
        return {"tp": tp_at(x, y + step)}

    def small_block(da, db):
        return chip_at(x + da + core * (db - da), y + db + core * (da - db))

    def small_near(da, db):
        return {"tp": small_block(da, db) * 2 + core}

    first = core == 0
    own_feat = pl.ds(pl.multiple_of(core * HEADW, HEADW), HEADW)
    oth_feat = pl.ds(pl.multiple_of((1 - core) * HEADW, HEADW), HEADW)

    def tokens(half, b):
        return pl.ds(pl.multiple_of(half * HALF + b * QBLK, QBLK), QBLK)

    ORDER = (0, 1, 2, 5, 6, 7, 3, 4)

    def w_rows(p):
        return pl.ds(pl.multiple_of(p * LANES + core * HEADW, HEADW), HEADW)

    load_x = [
        pltpu.make_async_copy(res.at[:, tokens(core, b)], xg.at[chip, b, own_feat], loads.at[0]) for b in ORDER
    ]
    load_w = [pltpu.make_async_copy(wqkv.at[p], wraw.at[w_rows(p)], loads.at[1]) for p in range(3)]
    load_o = pltpu.make_async_copy(wout, wo.at[own_feat], loads.at[2])
    load_fi = pltpu.make_async_copy(ffi, fi, loads.at[3])
    load_fo = pltpu.make_async_copy(ffo, fo, loads.at[4])
    for copy in load_x + load_w:
        copy.start()
    load_o.start()
    load_small = [
        pltpu.make_async_copy(src, dst, loads.at[6 + i])
        for i, (src, dst) in enumerate(((gain_a_in, gain_a), (gain_f_in, gain_f), (route_in, route)))
    ]
    for copy in load_small:
        copy.start()

    other = tp + 1 - 2 * core
    prev_dev = {"seq": lax.rem(z + 3 + core, 4), "tp": other}
    next_dev = {"seq": lax.rem(z + core, 4), "tp": other}
    z_peer = {"seq": lax.rem(z + 3 + 2 * core, 4), "tp": other}
    barrier = pltpu.get_barrier_semaphore()
    peers = [near(0, 0, 1), near(0, 0, -1), near(0, 1, 1), near(0, 1, -1), partner, z_peer]
    for dev in peers:
        pl.semaphore_signal(barrier, inc=1, device_id=dev, device_id_type=MESH)
    pl.semaphore_wait(barrier, len(peers))

    swap_x = [
        remote(
            res.at[:, tokens(1 - core, b)], xg.at[chip, b, own_feat], sends.at[0],
            recvs.at[1 if b in (3, 4) else 0], partner,
        )
        for b in ORDER
    ]
    swap_w = [
        remote(wqkv.at[p], wraw.at[w_rows(p)], sends.at[1], recvs.at[2], partner) for p in range(3)
    ]
    swap_o = remote(wout, wo.at[own_feat], sends.at[2], recvs.at[3], partner)
    for copy in swap_x + swap_w:
        copy.start()
    swap_o.start()

    def g_item(c, h, item, d, piece=None):
        s = SIGN[d]
        index, part, axis = {
            0: (block(h, 0, 0), None, 0),
            1: (block(h, 0, 0), None, 1),
            2: (block(h, -s, 0), d, 0),
            3: (block(h, -1, 0), None, 1),
            4: (block(h, 1, 0), None, 1),
            5: (block(h, 0, -s), d, 1),
            6: (block(h, 2, 0), None, 1),
            7: (block(h, -1, -s), d, 1),
            8: (block(h, 1, -s), d, 1),
            9: (block(h, 2, -s), d, 1),
        }[item]
        feats = pl.ds(0, LANES) if part is None else pl.ds(part * HEADW, HEADW)
        if piece is not None:
            feats = (own_feat, oth_feat)[piece]
        start, count = CHUNK[c][h]
        src = xg.at[index, pl.ds(start, count), feats]
        return remote(src, src, sends.at[3], grecv.at[c, item], near(h, axis, s))

    both_hd = [(h, d) for h in range(2) for d in range(2)]

    def g_start(c, item, piece=None):
        for h, d in both_hd:
            g_item(c, h, item, d, piece).start()

    def g_wait(c, item):
        count = CHUNK[c][0][1] * 2
        if item in (0, 1, 3, 4, 6):
            arrived(grecv.at[c, item], xg.at[0:2, 0:count])
        else:
            arrived(grecv.at[c, item], xg.at[0, 0:count])

    pltpu.make_async_copy(xg.at[0, 0:4], xg.at[0, 0:4], loads.at[0]).wait()
    g_start(0, 0, 0)
    g_start(0, 1, 0)
    arrived(recvs.at[0], xg.at[0, 0:3])
    g_start(0, 0, 1)
    g_start(0, 1, 1)
    arrived(recvs.at[1], xg.at[0, 0])
    load_fi.start()
    load_fo.start()

    for copy in load_small:
        copy.wait()

    pltpu.make_async_copy(wraw.at[0 : 3 * HEADW], wraw.at[0 : 3 * HEADW], loads.at[1]).wait()
    arrived(recvs.at[2], wraw.at[0 : 3 * HEADW])
    for k in range(CHIPS):
        cols = slice(k * LANES, (k + 1) * LANES)
        w2[k] = (wraw[:, cols].astype(F32) * gain_a[cols].astype(F32).reshape(1, LANES)).astype(BF16)

    g_wait(0, 0)
    g_start(0, 2)
    g_start(0, 3)
    g_start(0, 4)
    g_start(1, 0)
    g_start(1, 1)

    acc[...] = jnp.zeros_like(acc)
    ssq[...] = jnp.zeros_like(ssq)

    def qkv_pair(i1, i2, pairs):
        wpair = jnp.concatenate([w2[i1], w2[i2]], axis=1)
        for u in pairs:
            b1, b2 = PAIRS[u]
            x1 = jnp.concatenate([xg[i1, b1], xg[i1, b2]], axis=1)
            x2 = jnp.concatenate([xg[i2, b1], xg[i2, b2]], axis=1)
            xx = jnp.concatenate([x1, x2], axis=0)
            acc[u] += dot(wpair, xx)
            f = xx.astype(F32)
            ssq[u] += jnp.sum((f * f).reshape(2 * LANES // 8, 8, QUART), axis=0)

    def group0(pairs):
        qkv_pair(chip_at(x - 1, y), chip_at(x + 1, y), pairs)
        qkv_pair(chip_at(x, y - 1), chip_at(x, y + 1), pairs)

    def group1(pairs):
        qkv_pair(chip_at(x - 1, y - 1), chip_at(x + 1, y - 1), pairs)
        qkv_pair(chip_at(x - 1, y + 1), chip_at(x + 1, y + 1), pairs)
        qkv_pair(chip_at(x + 2, y), chip_at(x, y + 2), pairs)

    def group2(pairs):
        qkv_pair(chip_at(x + 2, y - 1), chip_at(x + 2, y + 1), pairs)
        qkv_pair(chip_at(x - 1, y + 2), chip_at(x + 1, y + 2), pairs)

    def group3(pairs):
        qkv_pair(chip, chip_at(x + 2, y + 2), pairs)

    EARLY = (0, 1, 2)
    LATE = (3,)

    row = route[...].astype(F32)
    r_i = lax.broadcasted_iota(jnp.int32, (CAP, CAP), 0)
    c_i = lax.broadcasted_iota(jnp.int32, (CAP, CAP), 1)
    col = jnp.sum(jnp.where(r_i == c_i, row, 0.0), axis=1, keepdims=True)
    lane = lax.broadcasted_iota(jnp.int32, (CAP, TOK), 1).astype(F32)
    oh[...] = jnp.where(lane == col, 1.0, 0.0).astype(BF16)
    k_i = lax.broadcasted_iota(jnp.int32, (3 * QBLK, QBLK), 0) - QBLK
    q_i = lax.broadcasted_iota(jnp.int32, (3 * QBLK, QBLK), 1)
    band = jnp.where(jnp.abs(q_i - k_i) <= RADIUS, 0.0, NEG)
    bias[0] = band + jnp.where(k_i < 0, jnp.where(z + core == 0, NEG, 0.0), 0.0)
    bias[1] = band
    bias[2] = band + jnp.where(k_i >= QBLK, jnp.where(z + core == 4, NEG, 0.0), 0.0)
    load_o.wait()
    arrived(recvs.at[3], wo.at[0:HEADW])
    for k in range(CHIPS):
        at = slice(k * LANES, (k + 1) * LANES)
        wot[at] = wo[:, at].astype(F32).T.astype(BF16)

    g_wait(0, 1)
    g_start(0, 5)
    qkv_pair(chip_at(x - 1, y), chip_at(x + 1, y), EARLY)
    g_wait(0, 2)
    g_start(0, 6)
    qkv_pair(chip_at(x, y - 1), chip_at(x, y + 1), EARLY)
    g_wait(0, 3)
    g_start(0, 7)
    g_wait(0, 4)
    g_start(0, 8)
    g_wait(1, 0)
    g_start(1, 2)
    g_start(1, 3)
    g_start(1, 4)

    mine_r = pl.ds(pl.multiple_of(core * CAPC, 16), CAPC)
    theirs_r = pl.ds(pl.multiple_of((1 - core) * CAPC, 16), CAPC)

    def quart_of(half, q):
        return pl.ds(pl.multiple_of(half * HALF + q * QUART, QUART), QUART)

    def pick(block_of):
        total = jnp.zeros((CAP, LANES), F32)
        for q in range(4):
            total = total + dot_nt(oh[:, quart_of(core, q)], block_of(q))
        return total.astype(BF16)

    pk[0] = pick(lambda q: jnp.concatenate([xg[chip, 2 * q], xg[chip, 2 * q + 1]], axis=1))
    swap_r = [
        remote(pk.at[i, theirs_r], px.at[i], sends.at[4], recvs.at[4 + i], partner) for i in range(2)
    ]
    swap_r[0].start()

    g_wait(0, 5)
    group1(EARLY)
    g_wait(0, 6)
    g_start(0, 9)
    g_wait(1, 1)
    g_start(1, 5)
    group0(LATE)
    g_wait(0, 7)
    g_wait(0, 8)
    g_wait(1, 2)
    g_start(1, 6)
    g_wait(1, 3)
    g_start(1, 7)
    g_wait(1, 4)
    g_start(1, 8)
    group2(EARLY)
    g_wait(0, 9)
    group3(EARLY)

    def finish_qkv(u):
        scale = lax.rsqrt(jnp.sum(ssq[u], axis=0, keepdims=True) * (1.0 / FEAT) + EPS)
        query = (acc[u, 0:LANES] * scale).astype(BF16).astype(F32) * (1.0 / HEADW**0.5)
        keys = (acc[u, LANES : 2 * LANES] * scale).T.astype(BF16)
        vals = (acc[u, 2 * LANES :] * scale).astype(BF16)
        for half in range(2):
            b = PAIRS[u][half]
            at = slice(half * QBLK, (half + 1) * QBLK)
            qt[:, b * QBLK : (b + 1) * QBLK] = query[:, at].astype(BF16)
            kvb[1 + b, 0] = keys[at]
            kvb[1 + b, 1] = vals[:, at]

    h_prev = remote(kvb.at[1], kvb.at[NBLK + 1], sends.at[5], recvs.at[6], prev_dev)
    h_next = remote(kvb.at[NBLK], kvb.at[0], sends.at[5], recvs.at[7], next_dev)
    finish_qkv(0)
    finish_qkv(1)
    h_prev.start()
    h_next.start()
    g_wait(1, 5)
    g_wait(1, 6)
    g_start(1, 9)
    finish_qkv(2)
    group1(LATE)

    def attend(i, kind):
        at = pl.ds(pl.multiple_of(i * QBLK, QBLK), QBLK)
        q = qt[:, at]
        zero = jnp.zeros((HEADW, QBLK), BF16)
        q2 = jnp.concatenate(
            [jnp.concatenate([q[:HEADW], zero], axis=0), jnp.concatenate([zero, q[HEADW:]], axis=0)], axis=1
        )
        keys = jnp.concatenate([kvb[i, 0], kvb[i + 1, 0], kvb[i + 2, 0]], axis=0)
        vals = jnp.concatenate([kvb[i, 1], kvb[i + 1, 1], kvb[i + 2, 1]], axis=1)
        b = bias[kind]
        s = dot(keys, q2) + jnp.concatenate([b, b], axis=1)
        e = jnp.exp(s - jnp.max(s, axis=0, keepdims=True))
        total = jnp.sum(e, axis=0, keepdims=True)
        o = dot(vals, e.astype(BF16)) / total
        ctx[:, at] = jnp.concatenate([o[:HEADW, :QBLK], o[HEADW:, QBLK:]], axis=0).astype(BF16)

    attend(1, 1)
    attend(NBLK - 2, 1)
    g_wait(1, 7)
    g_wait(1, 8)
    group2(LATE)
    arrived(recvs.at[6], kvb.at[0])
    arrived(recvs.at[7], kvb.at[0])
    attend(0, 0)
    attend(NBLK - 1, 2)

    def wot_rows(index):
        return wot[pl.ds(pl.multiple_of(index * LANES, LANES), LANES), :]

    def project(e, step):
        for h in range(2):
            q = SETS[e][h]
            rhs = ctx[:, q * QUART : (q + 1) * QUART]
            for pair in ((2, -1), (1, 0)):
                i1 = block(h, pair[0], step)
                i2 = block(h, pair[1], step)
                o = dot(jnp.concatenate([wot_rows(i1), wot_rows(i2)], axis=0), rhs).astype(BF16)
                pb[i1, q] = o[:LANES]
                pb[i2, q] = o[LANES:]

    def feats_of(part):
        return slice(part * HEADW, (part + 1) * HEADW)

    def r1_copy(e, h, j, kind, d):
        s = SIGN[d]
        db, part = ((2, d), (s, d), (s, 1 - d))[kind]
        src = pb.at[block(h, OFF[j], db), SETS[e][h], feats_of(part)]
        sem = rrecv.at[e, j if kind == 0 else 4 + j]
        return remote(src, rx1.at[e, h, j, kind, d], sends.at[6], sem, near(h, 1, s))

    def r2_copy(e, h, kind, d):
        s = SIGN[d]
        da, part = ((2, d), (s, d), (s, 1 - d))[kind]
        src = pb.at[block(h, da, 0), SETS[e][h], feats_of(part)]
        sem = rrecv.at[e, 8 if kind == 0 else 9]
        return remote(src, rx2.at[e, h, kind, d], sends.at[6], sem, near(h, 0, s))

    def r1_start(e, j, kind):
        for h, d in both_hd:
            r1_copy(e, h, j, kind, d).start()

    def r2_start(e, kind):
        for h, d in both_hd:
            r2_copy(e, h, kind, d).start()

    def relay1(e, j):
        arrived(rrecv.at[e, j], xg.at[0, 0:4])
        for h, d in both_hd:
            index = block(h, OFF[j], SIGN[d])
            q, at = SETS[e][h], feats_of(d)
            pb[index, q, at] = (pb[index, q, at].astype(F32) + rx1[e, h, j, 0, d].astype(F32)).astype(BF16)
            r1_copy(e, h, j, 1, d).start()

    def relay2(e):
        arrived(rrecv.at[e, 8], xg.at[0, 0:4])
        for h, d in both_hd:
            index = block(h, SIGN[d], 0)
            q, at = SETS[e][h], feats_of(d)
            pb[index, q, at] = (pb[index, q, at].astype(F32) + rx2[e, h, 0, d].astype(F32)).astype(BF16)
            r2_copy(e, h, 1, d).start()

    def sum1(e, h, j, part):
        got = pb[block(h, OFF[j], 0), SETS[e][h], feats_of(part)].astype(F32)
        return got + rx1[e, h, j, 1, part].astype(F32) + rx1[e, h, j, 2, 1 - part].astype(F32)

    def total1(e, j):
        arrived(rrecv.at[e, 4 + j], xg.at[0])
        for h in range(2):
            for part in range(2):
                pb[block(h, OFF[j], 0), SETS[e][h], feats_of(part)] = sum1(e, h, j, part).astype(BF16)

    def last(e):
        arrived(rrecv.at[e, 7], xg.at[0])
        arrived(rrecv.at[e, 9], xg.at[0])
        for h in range(2):
            q = SETS[e][h]
            for part in range(2):
                at = feats_of(part)
                own = jnp.concatenate([xg[chip, 2 * q, at], xg[chip, 2 * q + 1, at]], axis=1)
                mixed = sum1(e, h, 3, part) + rx2[e, h, 1, part].astype(F32) + rx2[e, h, 2, 1 - part].astype(F32)
                upd[q, at] = (own.astype(F32) + mixed).astype(BF16)

    def s1_copy(n, t, j):
        src = sb.at[n, small_block(t, j)]
        return remote(src, rxa.at[n, t - 1, j], sends.at[7], s1recv.at[n, j], small_near(t, 0))

    def s2_copy(n, t):
        src = sb2.at[n, t]
        return remote(src, rxb.at[n, t - 1], sends.at[7], s2recv.at[n], small_near(0, t))

    def o_copy(t):
        dev = {"tp": small_block(0, t) * 2 + 1 - core}
        return remote(sb2.at[1, t], rxo.at[t], sends.at[11], recvs.at[9], dev)

    STEPS = (2, 1, 3)
    COLS = (2, 1, 3, 0)

    def small_start(n):
        for j in COLS:
            for t in STEPS:
                s1_copy(n, t, j).start()

    def small_mid(n):
        for j in COLS:
            total = sb[n, small_block(0, j)].astype(F32)
            arrived(s1recv.at[n, j], sb.at[n, 0:3])
            for t in STEPS:
                total = total + rxa[n, t - 1, j].astype(F32)
            sb2[n, j] = total.astype(BF16)
            if j > 0:
                s2_copy(n, j).start()
            if n == 1:
                o_copy(j).start()

    def small_end(n):
        total = sb2[n, 0].astype(F32)
        arrived(s2recv.at[n], sb.at[n, 0:3])
        for t in STEPS:
            total = total + rxb[n, t - 1].astype(F32)
        return total

    def a_copy(t, j):
        if t == 0:
            src = gp.at[chip, mine_r]
            return remote(src, src, sends.at[8], arecv.at[3 + j], small_near(0, j))
        src = gp.at[small_block(0, -j), mine_r]
        return remote(src, src, sends.at[8], arecv.at[j], small_near(t, 0))

    def f_copy(t, j):
        src = gp.at[small_block(-t, -j), mine_r]
        return remote(src, src, sends.at[9], recvs.at[8], partner)

    def gather_first():
        for j in STEPS:
            a_copy(0, j).start()
        for t in STEPS:
            a_copy(t, 0).start()
        f_copy(0, 0).start()

    def gather_second():
        for j in (1, 3, 2):
            arrived(arecv.at[3 + j], sb.at[0, 0])
            for t in STEPS:
                a_copy(t, j).start()
            f_copy(0, j).start()

    def gather_third():
        for j in (0, 1, 3, 2):
            arrived(arecv.at[j], sb.at[0, 0:3])
            for t in (1, 3, 2):
                f_copy(t, j).start()

    def gather_last():
        arrived(recvs.at[8], sb.at[0])

    project(0, 2)
    r1_start(0, 0, 0)
    r1_start(0, 1, 0)
    r1_start(0, 2, 0)
    project(0, 1)
    project(0, -1)
    r1_start(0, 0, 2)
    g_wait(1, 9)
    group3(LATE)
    finish_qkv(3)
    r1_start(0, 1, 2)
    attend(2, 1)
    attend(3, 1)
    attend(4, 1)
    attend(5, 1)
    pk[1] = pick(lambda q: ctx[:, q * QUART : (q + 1) * QUART])
    swap_r[1].start()
    relay1(0, 0)
    project(1, 2)
    r1_start(0, 2, 2)
    arrived(recvs.at[4], px.at[0])
    arrived(recvs.at[5], px.at[0])
    rows_ctx = (pk[1, mine_r].astype(F32) + px[1].astype(F32)).astype(BF16)
    for k in range(CHIPS // 2):
        o = dot(rows_ctx, wo[:, k * 256 : (k + 1) * 256]).astype(BF16)
        sb[0, 2 * k] = o[:, :LANES]
        sb[0, 2 * k + 1] = o[:, LANES:]
    small_start(0)
    r1_start(0, 3, 0)
    project(0, 0)
    relay1(0, 1)
    relay1(0, 2)
    project(1, 1)
    small_mid(0)
    total1(0, 0)
    r2_start(0, 0)
    r1_start(0, 3, 2)
    r1_start(1, 0, 0)
    project(1, -1)
    rows_new = pk[0, mine_r].astype(F32) + px[0].astype(F32) + small_end(0)
    gp[chip, mine_r] = rows_new.astype(BF16)
    gather_first()
    relay1(0, 3)
    total1(0, 1)
    total1(0, 2)
    r2_start(0, 2)
    r1_start(1, 0, 2)
    r1_start(1, 1, 0)
    project(1, 0)
    gather_second()
    relay1(1, 0)
    r1_start(1, 1, 2)
    r1_start(1, 2, 0)
    r1_start(1, 2, 2)
    gather_third()
    relay2(0)
    r1_start(1, 3, 0)
    relay1(1, 1)
    relay1(1, 2)
    total1(1, 0)
    r2_start(1, 0)
    gather_last()

    sq = jnp.zeros((CAP, LANES), F32)
    for k in range(CHIPS):
        v = gp[k].astype(F32)
        sq = sq + v * v
    scale = lax.rsqrt(jnp.sum(sq, axis=1, keepdims=True) * (1.0 / FEAT) + EPS)
    for k in range(CHIPS):
        at = slice(k * LANES, (k + 1) * LANES)
        nrm[:, at] = (gp[k].astype(F32) * scale * gain_f[at].astype(F32).reshape(1, LANES)).astype(BF16)

    r1_start(1, 3, 2)
    load_fi.wait()

    def ffn_in(n0, nw):
        rows_n = nrm[...]
        gate = dot(rows_n, fi[0, :, n0 : n0 + nw])
        up = dot(rows_n, fi[1, :, n0 : n0 + nw])
        hid[:, n0 : n0 + nw] = (gelu(gate) * up).astype(BF16)

    ffn_in(0, 256)
    total1(1, 1)
    total1(1, 2)
    r2_start(1, 2)
    ffn_in(256, 256)
    relay1(1, 3)
    ffn_in(512, 128)
    relay2(1)
    last(0)
    load_fo.wait()

    def c_copy(n):
        pair = pl.ds(2 * n, 2)
        return remote(pb2.at[pair, theirs_r], rxc.at[pair], sends.at[10], crecv.at[n // 2], partner)

    for n in range(CHIPS // 2):
        o = dot(hid[...], fo[:, n * 256 : (n + 1) * 256]).astype(BF16)
        pb2[2 * n] = o[:, :LANES]
        pb2[2 * n + 1] = o[:, LANES:]
        c_copy(n).start()
    for n in range(4):
        arrived(crecv.at[n], sb.at[0, 0:4])
        for k in range(4 * n, 4 * n + 4):
            sb[1, k] = (pb2[k, mine_r].astype(F32) + rxc[k].astype(F32)).astype(BF16)
    small_start(1)
    small_mid(1)
    last(1)
    swap_u = remote(upd.at[:, oth_feat], updx, sends.at[12], recvs.at[10], partner)
    swap_u.start()
    heavy = small_end(1)
    arrived(recvs.at[9], sb.at[0, 0:4])
    heavy_oth = rxo[0].astype(F32)
    for t in STEPS:
        heavy_oth = heavy_oth + rxo[t].astype(F32)
    for rows, base_slot, value in ((mine_r, core * CAPC, heavy), (theirs_r, (1 - core) * CAPC, heavy_oth)):
        slot = lax.broadcasted_iota(jnp.int32, (CAPC, LANES), 0) + base_slot
        value = jnp.where(slot < counts[z], value, 0.0)
        high = value.astype(BF16)
        low = (value - high.astype(F32)).astype(BF16)
        hv[rows, :] = jnp.concatenate(
            [
                jnp.where(first, high[:, :HEADW], high[:, HEADW:]),
                jnp.where(first, low[:, :HEADW], low[:, HEADW:]),
            ],
            axis=1,
        )

    arrived(recvs.at[10], updx)
    for q in range(4):
        for half, rows_now in ((core, upd[q, own_feat]), (1 - core, updx[q])):
            at = quart_of(half, q)
            added = dot_tn(hv[...], oh[:, at])
            fin[:, at] = (rows_now.astype(F32) + added[:HEADW] + added[HEADW:]).astype(BF16)
    save_out = pltpu.make_async_copy(fin, out, loads.at[5])
    save_out.start()

    left(0, xg.at[0, 0:4])
    left(1, wraw.at[0 : 3 * HEADW])
    left(2, wo.at[0:HEADW])
    left(3, xg.at[0:15])
    left(4, px)
    left(5, kvb.at[0:2])
    left(6, pb.at[0:15])
    left(7, sb.at[:, 0:15])
    left(8, sb.at[0, 0:15])
    left(9, sb.at[0])
    left(10, sb.at[1])
    left(11, sb.at[0, 0:4])
    left(12, updx)
    save_out.wait()


def local(
    residual, attn_gain, attn_in, attn_out, ffn_gain, ffn_in, ffn_out, route_rows, route_counts
):
    any_spec = pl.BlockSpec(memory_space=pl.ANY)
    vm = pltpu.VMEM
    dma = pltpu.SemaphoreType.DMA
    turned = pl.pallas_call(
        kernel,
        out_shape=jax.ShapeDtypeStruct((HEADW, TOK), BF16),
        in_specs=[any_spec] * 8
        + [pl.BlockSpec(memory_space=pltpu.SMEM)],
        out_specs=any_spec,
        scratch_shapes=[
            vm((FEAT,), BF16),
            vm((FEAT,), BF16),
            vm((1, CAP), jnp.int32),
            vm((4, HEADW, QUART), BF16),
            vm((3 * LANES, FEAT), BF16),
            vm((LANES, FEAT), BF16),
            vm((FEAT, LANES), BF16),
            vm((2, FEAT, FFU), BF16),
            vm((FFU, FEAT), BF16),
            vm((CHIPS, 3 * LANES, LANES), BF16),
            vm((CHIPS, NBLK, LANES, QBLK), BF16),
            vm((4, 3 * LANES, QUART), F32),
            vm((4, 8, QUART), F32),
            vm((LANES, HALF), BF16),
            vm((NBLK + 2, 2, QBLK, QBLK), BF16),
            vm((LANES, HALF), BF16),
            vm((3, 3 * QBLK, QBLK), F32),
            vm((CAP, TOK), BF16),
            vm((CHIPS, 4, LANES, QUART), BF16),
            vm((2, 2, 4, 3, 2, HEADW, QUART), BF16),
            vm((2, 2, 3, 2, HEADW, QUART), BF16),
            vm((4, LANES, QUART), BF16),
            vm((HEADW, TOK), BF16),
            vm((CHIPS, CAP, LANES), BF16),
            vm((2, CAP, LANES), BF16),
            vm((2, CAPC, LANES), BF16),
            vm((CAP, FEAT), BF16),
            vm((CAP, FFU), BF16),
            vm((CHIPS, CAP, LANES), BF16),
            vm((CHIPS, CAPC, LANES), BF16),
            vm((2, CHIPS, CAPC, LANES), BF16),
            vm((2, 3, SIDE, CAPC, LANES), BF16),
            vm((2, SIDE, CAPC, LANES), BF16),
            vm((2, 3, CAPC, LANES), BF16),
            vm((SIDE, CAPC, LANES), BF16),
            vm((CAP, LANES), BF16),
            dma((9,)),
            dma((13,)),
            dma((11,)),
            dma((2, 10)),
            dma((2, 10)),
            dma((2, SIDE)),
            dma((2,)),
            dma((7,)),
            dma((4,)),
        ],
        compiler_params=pltpu.CompilerParams(
            collective_id=0, has_side_effects=True, vmem_limit_bytes=62 * 1024 * 1024
        ),
        name="layer",
    )(
        residual.T, attn_in.transpose(0, 2, 1), attn_out, ffn_in, ffn_out, attn_gain, ffn_gain, route_rows, route_counts
    )
    return turned.T


def solution(mesh):
    in_specs = (
        P("seq", "tp"),
        P(),
        P(None, None, "tp"),
        P("tp", None),
        P(),
        P(None, None, "tp"),
        P("tp", None),
        P("seq", None),
        P(),
    )
    out_specs = P("seq", "tp")
    return jax.shard_map(local, mesh=mesh, in_specs=in_specs, out_specs=out_specs, check_vma=False)
```
